32 devices in a mesh: dp: 2 (over core), row: 4 (over y, x), col: 4 (over z).
Axes of the slice: x: 2, y: 2, z: 4, core: 2. Of those that a mesh axis runs over, the one named last changes fastest.
Arguments:
- tokens: bfloat16 [768, 32768], P('col', ('dp', 'row')), may hold values from -6 to 6
- w_qkv: bfloat16 [768, 3, 768], P(('dp', 'row'), None, 'col'), may hold values from -0.3125 to 0.3125
- bias_qv: float32 [2, 768], P(None, 'col'), may hold values from -3 to 3
- w_attn_out: bfloat16 [768, 768], P(('dp', 'row'), 'col'), may hold values from -0.875 to 0.875
- bias_attn_out: float32 [768], P('col'), may hold values from -3 to 3
- w_in: bfloat16 [768, 3072], P(('dp', 'row'), 'col'), may hold values from -0.21875 to 0.21875
- bias_in: float32 [3072], P('col'), may hold values from -3 to 3
- w_out: bfloat16 [768, 3072], P(('dp', 'row'), 'col'), may hold values from -0.21875 to 0.21875
- bias_out: float32 [768], P('col'), may hold values from -3 to 3
- norm_gains: float32 [2, 768], P(None, 'col'), may hold values from 0.5 to 1.5
- norm_biases: float32 [2, 768], P(None, 'col'), may hold values from -3 to 3
- seq_lengths: int32 [32], P(('dp', 'row')), may hold values from 256 to 1024, as said below
- seq_offsets: int32 [32], P(('dp', 'row')), may hold values from 0 to 768, as said below
- cotangent: bfloat16 [768, 32768], P('col', ('dp', 'row')), may hold values from -6 to 6
Outputs:
- activations: float32 [768, 32768], P('col', ('dp', 'row'))
- token_grad: float32 [768, 32768], P('col', ('dp', 'row'))
- grad_qkv: float32 [768, 3, 768], P(('dp', 'row'), None, 'col')
- grad_bias_qv: float32 [2, 768], P(None, 'col')
- grad_attn_out: float32 [768, 768], P(('dp', 'row'), 'col')
- grad_bias_attn_out: float32 [768], P('col')
- grad_in: float32 [768, 3072], P(('dp', 'row'), 'col')
- grad_bias_in: float32 [3072], P('col')
- grad_out: float32 [768, 3072], P(('dp', 'row'), 'col')
- grad_bias_out: float32 [768], P('col')
- grad_norm_gains: float32 [2, 768], P(None, 'col')
- grad_norm_biases: float32 [2, 768], P(None, 'col')
The draws below stay inside these ranges and needn't reach their ends.
Inputs may be any that keep to these rules, and one draw needn't show every extreme that they name: seq_lengths[j] is the length of the one sequence of window j (tokens j * 1024 to (j + 1) * 1024 - 1); 1024 and 256 occur in every draw. seq_offsets[j] + seq_lengths[j] <= 1024: the sequence lies inside its window, the rest of the window is padding.
All inputs are finite; a program needn't handle non-finite values.
Results may differ from the reference program's by a relative error of at most 0.014.
The reference program's roundings to bfloat16 on the way count: a program that leaves them out, or rounds other values in their place, can miss the bound.
Values may be sent and summed in bfloat16 or wider, within the bound.
A program may use at most 192 MiB of HBM per device.

```python
import jax
import jax.numpy as jnp
from jax import lax

D = 768
HEADS = 12
HEAD_DIM = 64
FF = 3072
PACK = 2048
SEQ_MAX = 1024
MIN_LEN = 256
TOKENS = 32768


def draw_layout(key):
    seq_count = TOKENS // SEQ_MAX
    lengths = jax.random.randint(jax.random.fold_in(key, 11), (seq_count,), MIN_LEN, SEQ_MAX + 1)
    lengths = lengths.at[0].set(SEQ_MAX).at[1].set(MIN_LEN)
    offsets = jax.random.randint(jax.random.fold_in(key, 12), (seq_count,), 0, SEQ_MAX - lengths + 1)
    offsets = offsets.at[1].set(SEQ_MAX - MIN_LEN)
    return (lengths.astype(jnp.int32), offsets.astype(jnp.int32))


def draw_seq_lengths(key, part):
    return draw_layout(key)[0]


def draw_seq_offsets(key, part):
    return draw_layout(key)[1]


def level_of(key, shape, cuts, low, high):
    factor_of = 1.0
    for dim, parts in cuts:
        steps = jax.random.uniform(jax.random.fold_in(jax.random.fold_in(key, 6), dim), (parts,), jnp.float32, low / len(cuts), high / len(cuts))
        factor_of = factor_of * jnp.repeat(jnp.exp(steps), shape[dim] // parts).reshape((-1,) + (1,) * (len(shape) - 1 - dim))
    return factor_of


def noise(stream_key, shape, width, most, cuts=(), held_as=jnp.bfloat16):
    values = width * jax.random.normal(stream_key, shape, jnp.float32)
    if cuts:
        values = values * level_of(stream_key, shape, cuts, -0.22, 0.18)
    return jnp.clip(values, -most, most).astype(held_as)


def setup_inputs(seed: int = 0) -> dict:
    key_of = jax.random.split(jax.random.key(seed), 15)
    return {
        "tokens": noise(key_of[0], (D, TOKENS), 1.0, 6.0, ((0, 4), (1, 8))),
        "w_qkv": noise(key_of[1], (D, 3, D), (D // 2) ** -0.5, 0.3125, ((0, 8), (2, 4))),
        "bias_qv": noise(key_of[2], (2, D), 0.5, 3.0, ((1, 4),), jnp.float32),
        "w_attn_out": noise(key_of[3], (D, D), (D // 16) ** -0.5, 0.875, ((0, 8), (1, 4))),
        "bias_attn_out": noise(key_of[4], (D,), 0.5, 3.0, ((0, 4),), jnp.float32),
        "w_in": noise(key_of[5], (D, FF), D ** -0.5, 0.21875, ((0, 8), (1, 4))),
        "bias_in": noise(key_of[6], (FF,), 0.5, 3.0, ((0, 4),), jnp.float32),
        "w_out": noise(key_of[7], (D, FF), (FF // 4) ** -0.5, 0.21875, ((0, 8), (1, 4))),
        "bias_out": noise(key_of[8], (D,), 0.5, 3.0, ((0, 4),), jnp.float32),
        "norm_gains": jnp.clip(0.5 + 1.0 * jax.random.uniform(key_of[9], (2, D), jnp.float32) ** level_of(key_of[9], (2, D), ((1, 4),), -0.2, 0.2), 0.5, 1.5),
        "norm_biases": noise(key_of[10], (2, D), 0.5, 3.0, ((1, 4),), jnp.float32),
        "seq_lengths": draw_seq_lengths(jax.random.fold_in(key_of[14], 71), 0),
        "seq_offsets": draw_seq_offsets(jax.random.fold_in(key_of[14], 71), 0),
        "cotangent": noise(key_of[13], (D, TOKENS), 1.0, 6.0, ((0, 4), (1, 8))),
    }


@jax.custom_vjp
def low(v):
    return lax.optimization_barrier(v.astype(jnp.bfloat16)).astype(jnp.float32)

@jax.custom_vjp
def low_back(v):
    return v

def low_keep(v):
    return (low(v), None)

def low_pass(kept, grad):
    return (grad,)

def back_keep(v):
    return (v, None)

def back_low(kept, grad):
    return (low(grad),)
low.defvjp(low_keep, low_pass)
low_back.defvjp(back_keep, back_low)
EPSILON = 1e-12
HIGHEST = lax.Precision.HIGHEST

def layer_norm(values, gain_row, shift_row):
    average = lax.optimization_barrier(jnp.mean(values, axis=-1, keepdims=True))
    centred = values - average
    spread = lax.optimization_barrier(jnp.mean(centred * centred, axis=-1, keepdims=True))
    return centred * lax.rsqrt(spread + EPSILON) * gain_row + shift_row

def attend_window(queries, key_rows, values, live_mask):
    scores = jnp.einsum('qhe,khe->hqk', queries, key_rows, precision=HIGHEST) * HEAD_DIM ** (-0.5)
    scores = low_back(scores)
    allowed = live_mask[:, None] == live_mask[None, :]
    scores = jnp.where(allowed[None], scores, -1e+30)
    largest = lax.optimization_barrier(jnp.max(scores, axis=-1, keepdims=True))
    exponent = jnp.exp(scores - largest)
    soft_weights = exponent / lax.optimization_barrier(jnp.sum(exponent, axis=-1, keepdims=True))
    return jnp.einsum('hqk,khe->qhe', low(soft_weights), values, precision=HIGHEST)

def layer_pack(params, token_rows, lengths, offsets):
    w_qkv, bias_qv, w_attn_out, bias_attn_out, w_in, bias_in, w_out, bias_out, gains, shifts = params
    windows = PACK // SEQ_MAX
    places = jnp.arange(SEQ_MAX, dtype=jnp.int32)
    live_mask = (places[None, :] >= offsets[:, None]) & (places[None, :] < offsets[:, None] + lengths[:, None])
    live_rows = live_mask.reshape(PACK).astype(jnp.float32)[:, None]
    projected = low_back(jnp.einsum('td,dke->tke', token_rows, w_qkv, precision=HIGHEST))
    queries = low(projected[:, 0] + bias_qv[0])
    key_rows = low(projected[:, 1])
    values = low(projected[:, 2] + bias_qv[1])
    window_shape = (windows, SEQ_MAX, HEADS, HEAD_DIM)
    attend = jax.checkpoint(lambda pieces: attend_window(pieces[0], pieces[1], pieces[2], pieces[3]))
    attended = lax.map(attend, (queries.reshape(window_shape), key_rows.reshape(window_shape), values.reshape(window_shape), live_mask))
    attended = low(low_back(attended.reshape(PACK, D)))
    branch = low_back(jnp.dot(attended, w_attn_out.T, precision=HIGHEST)) + bias_attn_out
    normed = layer_norm(token_rows + branch, gains[0], shifts[0])
    hidden = low_back(jnp.dot(low(normed), w_in, precision=HIGHEST)) + bias_in
    active = low(jax.nn.gelu(hidden, approximate=False))
    second = low_back(jnp.dot(active, w_out.T, precision=HIGHEST)) + bias_out
    result = layer_norm(normed + second, gains[1], shifts[1])
    return result * live_rows

def reference(tokens, w_qkv, bias_qv, w_attn_out, bias_attn_out, w_in, bias_in, w_out, bias_out, norm_gains, norm_biases, seq_lengths, seq_offsets, cotangent):
    params = tuple((array.astype(jnp.float32) for array in (w_qkv, bias_qv, w_attn_out, bias_attn_out, w_in, bias_in, w_out, bias_out, norm_gains, norm_biases)))
    pack_count = TOKENS // PACK
    windows = PACK // SEQ_MAX
    token_rows = tokens.astype(jnp.float32).T.reshape(pack_count, PACK, D)
    lengths = seq_lengths.astype(jnp.int32).reshape(pack_count, windows)
    offsets = seq_offsets.astype(jnp.int32).reshape(pack_count, windows)

    def forward(params, token_rows):

        def pack_step(carried, pieces):
            return (carried, layer_pack(params, pieces[0], pieces[1], pieces[2]))
        unused, results = lax.scan(pack_step, jnp.zeros((), jnp.float32), (token_rows, lengths, offsets))
        return results
    results, pullback = jax.vjp(forward, params, token_rows)
    gradients, row_grads = pullback(cotangent.astype(jnp.float32).T.reshape(pack_count, PACK, D))
    return (results.reshape(TOKENS, D).T, row_grads.reshape(TOKENS, D).T, gradients[0], gradients[1], gradients[2], gradients[3], gradients[4], gradients[5], gradients[6], gradients[7], gradients[8], gradients[9])
```

```python
import jax
import jax.numpy as jnp
from jax import lax
from jax.sharding import PartitionSpec as P

HEAD_DIM = 64
SEQ_MAX = 1024
EPSILON = 1e-12
ROWS = ("dp", "row")
ALL = ("dp", "row", "col")
BF = jnp.bfloat16
F32 = jnp.float32


def dot_nn(a, b):
    return lax.dot_general(a, b, (((1,), (0,)), ((), ())), preferred_element_type=F32)


def dot_tn(a, b):
    return lax.dot_general(a, b, (((0,), (0,)), ((), ())), preferred_element_type=F32)


def dot_nt(a, b):
    return lax.dot_general(a, b, (((1,), (1,)), ((), ())), preferred_element_type=F32)


def norm_forward(values, gain, shift):
    average = jnp.mean(values, axis=0, keepdims=True)
    centred = values - average
    spread = jnp.mean(centred * centred, axis=0, keepdims=True)
    inverse = lax.rsqrt(spread + EPSILON)
    scaled = centred * inverse
    return scaled * gain[:, None] + shift[:, None], scaled, inverse


def norm_backward(upstream, scaled, inverse, gain):
    weighted = upstream * gain[:, None]
    first = jnp.mean(weighted, axis=0, keepdims=True)
    second = jnp.mean(weighted * scaled, axis=0, keepdims=True)
    return inverse * (weighted - first - scaled * second)


def masked_scores(queries, keys, live):
    scores = jnp.einsum("hek,heq->hkq", keys, queries, preferred_element_type=F32)
    scores = scores * HEAD_DIM ** (-0.5)
    return jnp.where((live[:, None] == live[None, :])[None], scores, -1e30)


def attend_forward(queries, keys, values, live):
    scores = masked_scores(queries, keys, live)
    largest = jnp.max(scores, axis=1, keepdims=True)
    exponent = jnp.exp(scores - largest)
    total = jnp.sum(exponent, axis=1, keepdims=True)
    weights = (exponent / total).astype(BF)
    out = jnp.einsum("hek,hkq->heq", values, weights, preferred_element_type=F32)
    return out, largest + jnp.log(total)


def attend_backward(queries, keys, values, live, log_total, d_attended):
    scores = masked_scores(queries, keys, live)
    weights = jnp.exp(scores - log_total)
    d_weights = jnp.einsum("hek,heq->hkq", values, d_attended, preferred_element_type=F32)
    centre = jnp.sum(weights * d_weights, axis=1, keepdims=True)
    d_scores = (weights * (d_weights - centre)).astype(BF)
    scale = HEAD_DIM ** (-0.5)
    d_q = jnp.einsum("hek,hkq->heq", keys, d_scores, preferred_element_type=F32) * scale
    d_k = jnp.einsum("heq,hkq->hek", queries, d_scores, preferred_element_type=F32) * scale
    d_v = jnp.einsum("heq,hkq->hek", d_attended, weights.astype(BF), preferred_element_type=F32)
    return d_q, d_k, d_v


def local(
    tokens, w_qkv, bias_qv, w_attn_out, bias_attn_out, w_in, bias_in, w_out, bias_out,
    norm_gains, norm_biases, seq_lengths, seq_offsets, cotangent,
):
    cols = lax.axis_size("col")
    col = lax.axis_index("col")
    groups = lax.axis_size("dp") * lax.axis_size("row")

    def gather(shard):
        rows, width = shard.shape
        full = lax.all_gather(shard, ALL, axis=0, tiled=False)
        full = full.reshape(groups, cols, rows, width).transpose(0, 2, 1, 3)
        return full.reshape(groups * rows, cols * width)

    def scatter(grad):
        rows, width = grad.shape[0] // groups, grad.shape[1] // cols
        parts = grad.astype(BF).reshape(groups, rows, cols, width).transpose(0, 2, 1, 3)
        parts = parts.reshape(groups * cols * rows, width)
        return lax.psum_scatter(parts, ALL, scatter_dimension=0, tiled=True).astype(F32)

    d_local = w_qkv.shape[0]
    width = w_qkv.shape[2]
    d = d_local * groups
    heads = d // HEAD_DIM

    def whole_vector(v):
        return lax.all_gather(v, "col", axis=v.ndim - 1, tiled=True)

    full_q = gather(w_qkv[:, 0])
    full_k = gather(w_qkv[:, 1])
    full_v = gather(w_qkv[:, 2])
    full_qkv = jnp.concatenate([full_q, full_k, full_v], axis=1)
    full_attn_out = gather(w_attn_out)
    full_in = gather(w_in)
    full_out = gather(w_out)
    bias_qv = whole_vector(bias_qv)
    bias_attn_out = whole_vector(bias_attn_out)
    bias_in = whole_vector(bias_in)
    bias_out = whole_vector(bias_out)
    gains = whole_vector(norm_gains)
    shifts = whole_vector(norm_biases)

    def to_window(a):
        return lax.all_to_all(a, "col", split_axis=1, concat_axis=0, tiled=True)

    def from_window(a):
        return lax.all_to_all(a.astype(BF), "col", split_axis=0, concat_axis=1, tiled=True).astype(F32)

    x = to_window(tokens)
    up = to_window(cotangent)
    length = lax.dynamic_index_in_dim(seq_lengths, col, keepdims=False)
    offset = lax.dynamic_index_in_dim(seq_offsets, col, keepdims=False)
    places = jnp.arange(SEQ_MAX, dtype=jnp.int32)
    live_mask = (places >= offset) & (places < offset + length)
    live = live_mask.astype(F32)[None, :]

    proj = dot_tn(full_qkv, x)
    queries = (proj[:d] + bias_qv[0][:, None]).astype(BF).reshape(heads, HEAD_DIM, SEQ_MAX)
    keys = proj[d : 2 * d].astype(BF).reshape(heads, HEAD_DIM, SEQ_MAX)
    values = (proj[2 * d :] + bias_qv[1][:, None]).astype(BF).reshape(heads, HEAD_DIM, SEQ_MAX)
    def forward_group(group):
        return attend_forward(group[0], group[1], group[2], live_mask)

    def split_heads(a):
        return a.reshape(cols, heads // cols, *a.shape[1:])

    def join_heads(a):
        return a.reshape(heads, *a.shape[2:])

    groups_in = tuple(split_heads(a) for a in (queries, keys, values))
    attended, log_total = lax.map(forward_group, groups_in)
    attended = join_heads(attended)
    attended = attended.astype(BF).reshape(d, SEQ_MAX)
    first_sum = x.astype(F32) + dot_nn(full_attn_out, attended) + bias_attn_out[:, None]
    normed, xhat1, rstd1 = norm_forward(first_sum, gains[0], shifts[0])
    normed_low = normed.astype(BF)
    hidden = dot_tn(full_in, normed_low) + bias_in[:, None]
    cdf = 0.5 * (1.0 + lax.erf(hidden * 0.5**0.5))
    active = (hidden * cdf).astype(BF)
    slope = cdf + hidden * jnp.exp(-0.5 * hidden * hidden) * 0.3989422804014327
    second_sum = normed + dot_nn(full_out, active) + bias_out[:, None]
    result, xhat2, rstd2 = norm_forward(second_sum, gains[1], shifts[1])
    activations = from_window(result * live)

    upstream = up.astype(F32) * live
    gain_two = jnp.sum(upstream * xhat2, axis=1)
    shift_two = jnp.sum(upstream, axis=1)
    d_second = norm_backward(upstream, xhat2, rstd2, gains[1])
    g_bias_out = jnp.sum(d_second, axis=1)
    d_second_low = d_second.astype(BF)
    g_out = scatter(dot_nt(d_second_low, active))
    d_hidden = dot_tn(full_out, d_second_low) * slope
    g_bias_in = jnp.sum(d_hidden, axis=1)
    d_hidden_low = d_hidden.astype(BF)
    g_in = scatter(dot_nt(normed_low, d_hidden_low))
    d_normed = d_second + dot_nn(full_in, d_hidden_low)
    gain_one = jnp.sum(d_normed * xhat1, axis=1)
    shift_one = jnp.sum(d_normed, axis=1)
    d_first = norm_backward(d_normed, xhat1, rstd1, gains[0])
    g_bias_attn = jnp.sum(d_first, axis=1)
    d_first_low = d_first.astype(BF)
    g_attn = scatter(dot_nt(d_first_low, attended))
    d_attended = dot_tn(full_attn_out, d_first_low).astype(BF).reshape(heads, HEAD_DIM, SEQ_MAX)
    def backward_group(group):
        return attend_backward(group[0], group[1], group[2], live_mask, group[3], group[4])

    d_q, d_k, d_v = lax.map(backward_group, (*groups_in, log_total, split_heads(d_attended)))
    d_q, d_k, d_v = d_q.reshape(d, -1), d_k.reshape(d, -1), d_v.reshape(d, -1)
    g_bias_q = jnp.sum(d_q, axis=1)
    g_bias_v = jnp.sum(d_v, axis=1)
    d_proj = jnp.concatenate([d_q, d_k, d_v], axis=0).astype(BF)
    grad = dot_nt(x, d_proj).reshape(d, 3, d)
    g_qkv = jnp.stack([scatter(grad[:, k]) for k in range(3)], axis=1)
    token_grad = from_window(d_first + dot_nn(full_qkv, d_proj))

    small = jnp.stack([g_bias_q, g_bias_v, g_bias_attn, g_bias_out, gain_one, gain_two, shift_one, shift_two])
    small = jnp.concatenate([small, g_bias_in.reshape(-1, d)], axis=0)
    small = lax.psum(small, ALL)
    own = lax.dynamic_slice_in_dim(small[:8], col * width, width, axis=1)
    hid = bias_in.shape[0] // cols
    own_in = lax.dynamic_slice_in_dim(small[8:].reshape(-1), col * hid, hid, axis=0)
    return (
        activations, token_grad, g_qkv, own[0:2], g_attn, own[2], g_in, own_in, g_out, own[3],
        own[4:6], own[6:8],
    )


def solution(mesh):
    return jax.shard_map(
        local,
        mesh=mesh,
        in_specs=(
            P("col", ROWS), P(ROWS, None, "col"), P(None, "col"), P(ROWS, "col"), P("col"),
            P(ROWS, "col"), P("col"), P(ROWS, "col"), P("col"), P(None, "col"), P(None, "col"),
            P(ROWS), P(ROWS), P("col", ROWS),
        ),
        out_specs=(
            P("col", ROWS), P("col", ROWS), P(ROWS, None, "col"), P(None, "col"), P(ROWS, "col"),
            P("col"), P(ROWS, "col"), P("col"), P(ROWS, "col"), P("col"), P(None, "col"), P(None, "col"),
        ),
        check_vma=False,
    )
```

```python
import jax
import jax.numpy as jnp
from jax import lax
from jax.experimental import pallas as pl
from jax.experimental.pallas import tpu as pltpu
from jax.sharding import PartitionSpec as P

HEAD_DIM = 64
SEQ_MAX = 1024
EPSILON = 1e-12
ROWS = ("dp", "row")
ALL = ("dp", "row", "col")
OWNERS = ("col", "dp", "row")
BF = jnp.bfloat16
F32 = jnp.float32
LOG2E = 1.4426950408889634
SCALE = HEAD_DIM ** (-0.5)
QBLOCK = 256
EXTRA = 16


def dot_nn(a, b):
    return lax.dot_general(a, b, (((1,), (0,)), ((), ())), preferred_element_type=F32)


def dot_tn(a, b):
    return lax.dot_general(a, b, (((0,), (0,)), ((), ())), preferred_element_type=F32)


def dot_nt(a, b):
    return lax.dot_general(a, b, (((1,), (1,)), ((), ())), preferred_element_type=F32)


def mean_rows(v):
    return jnp.mean(v, axis=0, keepdims=True)


def norm_forward(values, gain, shift):
    centred = values - mean_rows(values)
    inverse = lax.rsqrt(mean_rows(centred * centred) + EPSILON)
    scaled = centred * inverse
    return scaled * gain[:, None] + shift[:, None], scaled, inverse


def norm_backward(upstream, scaled, inverse, gain):
    weighted = upstream * gain[:, None]
    return inverse * (weighted - mean_rows(weighted) - scaled * mean_rows(weighted * scaled))


def stack_rows(rows, width):
    place = lax.broadcasted_iota(jnp.int32, (EXTRA, width), 0)
    out = jnp.zeros((EXTRA, width), F32)
    for i, row in enumerate(rows):
        out = jnp.where(place == i, row, out)
    return out.astype(BF)


def three_parts(row):
    high = row.astype(BF).astype(F32)
    middle = (row - high).astype(BF).astype(F32)
    return high, middle, row - high - middle


def attend_forward_kernel(q_ref, k_ref, v_ref, mask_ref, out_ref, total_ref):
    seq = q_ref.shape[-1]
    one = jnp.ones((1, seq), F32)
    keys = jnp.concatenate([k_ref[0, 0, 0], stack_rows([mask_ref[...]], seq)], axis=0).T
    queries = jnp.concatenate([q_ref[0, 0, 0], stack_rows([one], seq)], axis=0)
    values = v_ref[0, 0, 0]
    for j in range(seq // QBLOCK):
        cols = slice(j * QBLOCK, (j + 1) * QBLOCK)
        scores = dot_nn(keys, queries[:, cols])
        largest = jnp.max(scores, axis=0, keepdims=True)
        exponent = jnp.exp2((scores - largest) * (SCALE * LOG2E))
        total = jnp.sum(exponent, axis=0, keepdims=True)
        weights = (exponent * (1.0 / total)).astype(BF)
        out_ref[0, :, cols] = dot_nn(values, weights).astype(BF)
        total_ref[0, :, cols] = largest + jnp.log(total) * (1.0 / SCALE)


def attend_backward_kernel(
    q_ref, k_ref, v_ref, mask_ref, out_ref, total_ref, up_ref, grad_ref, bias_ref, dk_ref, dv_ref
):
    seq = q_ref.shape[-1]
    one = jnp.ones((1, seq), F32)
    keys = k_ref[0, 0, 0]
    queries = q_ref[0, 0, 0]
    up = up_ref[0]
    delta = jnp.sum(up.astype(F32) * out_ref[0].astype(F32), axis=0, keepdims=True)
    key_side = jnp.concatenate([keys, stack_rows([mask_ref[...], one, one, one], seq)], axis=0).T
    value_side = jnp.concatenate([v_ref[0, 0, 0], stack_rows([one, one, one], seq)], axis=0).T
    query_side = jnp.concatenate([queries, stack_rows([one, *three_parts(-total_ref[0])], seq)], axis=0)
    up_side = jnp.concatenate([up, stack_rows(three_parts(-delta), seq)], axis=0)
    lanes = 128
    sum_q = jnp.zeros((HEAD_DIM, lanes), F32)
    for j in range(seq // QBLOCK):
        cols = slice(j * QBLOCK, (j + 1) * QBLOCK)
        weights = jnp.exp2(dot_nn(key_side, query_side[:, cols]) * (SCALE * LOG2E))
        d_scores = (weights * dot_nn(value_side, up_side[:, cols])).astype(BF)
        d_q = dot_nn(keys, d_scores) * SCALE
        for part in range(QBLOCK // lanes):
            sum_q += d_q[:, part * lanes : (part + 1) * lanes]
        grad_ref[0, 0, 0, :, cols] = d_q.astype(BF)
        d_k = dot_nt(queries[:, cols], d_scores)
        d_v = dot_nt(up[:, cols], weights.astype(BF))
        if j == 0:
            dk_ref[...] = d_k
            dv_ref[...] = d_v
        else:
            dk_ref[...] += d_k
            dv_ref[...] += d_v
    grad_ref[0, 1, 0] = (dk_ref[...] * SCALE).astype(BF)
    grad_ref[0, 2, 0] = dv_ref[...].astype(BF)
    bias_ref[0, 0] = sum_q
    sum_v = jnp.zeros((HEAD_DIM, lanes), F32)
    for part in range(seq // lanes):
        sum_v += dv_ref[:, part * lanes : (part + 1) * lanes]
    bias_ref[0, 1] = sum_v


def projection_spec(which, per_col, seq):
    return pl.BlockSpec((1, 1, 1, HEAD_DIM, seq), lambda h: (h // per_col, which, h % per_col, 0, 0))


def head_spec(rows, seq):
    return pl.BlockSpec((1, rows, seq), lambda h: (h, 0, 0))


def attend_forward(qkv, mask):
    cols, _, per_col, _, seq = qkv.shape
    heads = cols * per_col
    return pl.pallas_call(
        attend_forward_kernel,
        grid=(heads,),
        in_specs=[projection_spec(k, per_col, seq) for k in range(3)]
        + [pl.BlockSpec((1, seq), lambda h: (0, 0))],
        out_specs=[head_spec(HEAD_DIM, seq), head_spec(1, seq)],
        out_shape=[
            jax.ShapeDtypeStruct((heads, HEAD_DIM, seq), BF),
            jax.ShapeDtypeStruct((heads, 1, seq), F32),
        ],
        cost_estimate=pl.CostEstimate(
            flops=heads * seq * seq * HEAD_DIM * 16, bytes_accessed=heads * seq * HEAD_DIM * 8,
            transcendentals=heads * seq * seq,
        ),
        name="attend_forward",
    )(qkv, qkv, qkv, mask)


def attend_backward(qkv, mask, attended, total, d_attended):
    cols, _, per_col, _, seq = qkv.shape
    heads = cols * per_col
    return pl.pallas_call(
        attend_backward_kernel,
        grid=(heads,),
        in_specs=[projection_spec(k, per_col, seq) for k in range(3)]
        + [pl.BlockSpec((1, seq), lambda h: (0, 0))]
        + [head_spec(HEAD_DIM, seq), head_spec(1, seq), head_spec(HEAD_DIM, seq)],
        out_specs=[
            pl.BlockSpec((1, 3, 1, HEAD_DIM, seq), lambda h: (h // per_col, 0, h % per_col, 0, 0)),
            pl.BlockSpec((1, 2, HEAD_DIM, 128), lambda h: (h, 0, 0, 0)),
        ],
        out_shape=[
            jax.ShapeDtypeStruct(qkv.shape, BF),
            jax.ShapeDtypeStruct((heads, 2, HEAD_DIM, 128), F32),
        ],
        scratch_shapes=[pltpu.VMEM((HEAD_DIM, seq), F32), pltpu.VMEM((HEAD_DIM, seq), F32)],
        cost_estimate=pl.CostEstimate(
            flops=heads * seq * seq * HEAD_DIM * 40, bytes_accessed=heads * seq * HEAD_DIM * 16,
            transcendentals=heads * seq * seq,
        ),
        name="attend_backward",
    )(qkv, qkv, qkv, mask, attended, total, d_attended)


def local(
    tokens, w_qkv, bias_qv, w_attn_out, bias_attn_out, w_in, bias_in, w_out, bias_out,
    norm_gains, norm_biases, seq_lengths, seq_offsets, cotangent,
):
    cols = lax.axis_size("col")
    col = lax.axis_index("col")
    rows, _, width = w_qkv.shape
    groups = lax.axis_size("dp") * lax.axis_size("row")
    d = rows * groups
    heads = d // HEAD_DIM
    hid = w_in.shape[1]

    def gather(shard):
        return lax.all_gather(shard, OWNERS, axis=0, tiled=True).reshape(cols, d, shard.shape[1])

    def scatter(grad):
        parts = grad.astype(BF).reshape(cols * d, grad.shape[2])
        return lax.psum_scatter(parts, OWNERS, scatter_dimension=0, tiled=True).astype(F32)

    w_mix = gather(jnp.concatenate([w_qkv.reshape(rows, 3 * width), w_attn_out], axis=1))
    full_in = gather(w_in)
    full_out = gather(w_out)
    full_qkv = w_mix[:, :, : 3 * width]
    full_attn = w_mix[:, :, 3 * width :]

    vectors = jnp.concatenate(
        [bias_qv, bias_attn_out[None], bias_out[None], norm_gains, norm_biases, bias_in.reshape(-1, width)], axis=0
    )
    vectors = lax.all_gather(vectors, "col", axis=0, tiled=False)
    bias_q, bias_v = vectors[:, 0], vectors[:, 1]
    bias_attn_out, bias_out = vectors[:, 2].reshape(d), vectors[:, 3].reshape(d)
    gains = [vectors[:, 4].reshape(d), vectors[:, 5].reshape(d)]
    shifts = [vectors[:, 6].reshape(d), vectors[:, 7].reshape(d)]
    bias_in = vectors[:, 8:].reshape(cols, hid)

    def to_window(a):
        return lax.all_to_all(a, "col", split_axis=1, concat_axis=0, tiled=True)

    def from_window(a):
        return lax.all_to_all(a.astype(BF), "col", split_axis=0, concat_axis=1, tiled=True).astype(F32)

    x = to_window(tokens)
    up = to_window(cotangent)
    length = lax.dynamic_index_in_dim(seq_lengths, col, keepdims=False)
    offset = lax.dynamic_index_in_dim(seq_offsets, col, keepdims=False)
    places = lax.broadcasted_iota(jnp.int32, (1, SEQ_MAX), 1)
    live_mask = (places >= offset) & (places < offset + length)
    live = live_mask.astype(F32)
    key_mask = jnp.where(live_mask, 0.0, -1e30).astype(F32)

    proj = jnp.einsum("cdn,dt->cnt", full_qkv, x, preferred_element_type=F32)
    shift_qkv = jnp.concatenate([bias_q, jnp.zeros_like(bias_q), bias_v], axis=1)
    qkv = (proj + shift_qkv[:, :, None]).astype(BF).reshape(cols, 3, width // HEAD_DIM, HEAD_DIM, SEQ_MAX)
    attended, total = attend_forward(qkv, key_mask)
    attended_cols = attended.reshape(cols, width, SEQ_MAX)
    first_sum = (
        x.astype(F32) + jnp.einsum("cde,cet->dt", full_attn, attended_cols, preferred_element_type=F32)
        + bias_attn_out[:, None]
    )
    normed, xhat1, rstd1 = norm_forward(first_sum, gains[0], shifts[0])
    normed_low = normed.astype(BF)
    hidden = jnp.einsum("cdf,dt->cft", full_in, normed_low, preferred_element_type=F32) + bias_in[:, :, None]
    cdf = 0.5 * (1.0 + lax.erf(hidden * 0.5**0.5))
    active = (hidden * cdf).astype(BF)
    slope = cdf + hidden * jnp.exp(-0.5 * hidden * hidden) * 0.3989422804014327
    second_sum = (
        normed + jnp.einsum("cdf,cft->dt", full_out, active, preferred_element_type=F32) + bias_out[:, None]
    )
    result, xhat2, rstd2 = norm_forward(second_sum, gains[1], shifts[1])
    activations = from_window(result * live)

    upstream = up.astype(F32) * live
    gain_two = jnp.sum(upstream * xhat2, axis=1)
    shift_two = jnp.sum(upstream, axis=1)
    d_second = norm_backward(upstream, xhat2, rstd2, gains[1])
    g_bias_out = jnp.sum(d_second, axis=1)
    d_second_low = d_second.astype(BF)
    g_out = scatter(jnp.einsum("dt,cft->cdf", d_second_low, active, preferred_element_type=F32))
    d_hidden = jnp.einsum("cdf,dt->cft", full_out, d_second_low, preferred_element_type=F32) * slope
    g_bias_in = jnp.sum(d_hidden, axis=2)
    d_hidden_low = d_hidden.astype(BF)
    g_in = scatter(jnp.einsum("dt,cft->cdf", normed_low, d_hidden_low, preferred_element_type=F32))
    d_normed = d_second + jnp.einsum("cdf,cft->dt", full_in, d_hidden_low, preferred_element_type=F32)
    gain_one = jnp.sum(d_normed * xhat1, axis=1)
    shift_one = jnp.sum(d_normed, axis=1)
    d_first = norm_backward(d_normed, xhat1, rstd1, gains[0])
    g_bias_attn = jnp.sum(d_first, axis=1)
    d_first_low = d_first.astype(BF)
    d_attended = jnp.einsum("cde,dt->cet", full_attn, d_first_low, preferred_element_type=F32).astype(BF)
    d_attended = d_attended.reshape(heads, HEAD_DIM, SEQ_MAX)
    grads, bias_sums = attend_backward(qkv, key_mask, attended, total, d_attended)
    d_proj = grads.reshape(cols, 3 * width, SEQ_MAX)
    bias_sums = jnp.sum(bias_sums, axis=3)
    g_bias_q, g_bias_v = bias_sums[:, 0].reshape(d), bias_sums[:, 1].reshape(d)
    g_attn = jnp.einsum("dt,cet->cde", d_first_low, attended_cols, preferred_element_type=F32)
    g_qkv = jnp.einsum("dt,cnt->cdn", x, d_proj, preferred_element_type=F32)
    g_mix = scatter(jnp.concatenate([g_qkv.astype(BF), g_attn.astype(BF)], axis=2))
    token_grad = from_window(d_first + jnp.einsum("cdn,cnt->dt", full_qkv, d_proj, preferred_element_type=F32))

    small = jnp.stack([g_bias_q, g_bias_v, g_bias_attn, g_bias_out, gain_one, gain_two, shift_one, shift_two])
    small = small.reshape(8, cols, width).transpose(1, 0, 2)
    small = jnp.concatenate([small, g_bias_in.reshape(cols, -1, width)], axis=1)
    small = lax.psum(small, ALL)
    own = lax.dynamic_index_in_dim(small, col, axis=0, keepdims=False)
    return (
        activations, token_grad, g_mix[:, : 3 * width].reshape(rows, 3, width), own[0:2],
        g_mix[:, 3 * width :], own[2], g_in, own[8:].reshape(hid), g_out, own[3], own[4:6], own[6:8],
    )


def solution(mesh):
    return jax.shard_map(
        local,
        mesh=mesh,
        in_specs=(
            P("col", ROWS), P(ROWS, None, "col"), P(None, "col"), P(ROWS, "col"), P("col"),
            P(ROWS, "col"), P("col"), P(ROWS, "col"), P("col"), P(None, "col"), P(None, "col"),
            P(ROWS), P(ROWS), P("col", ROWS),
        ),
        out_specs=(
            P("col", ROWS), P("col", ROWS), P(ROWS, None, "col"), P(None, "col"), P(ROWS, "col"),
            P("col"), P(ROWS, "col"), P("col"), P(ROWS, "col"), P("col"), P(None, "col"), P(None, "col"),
        ),
        check_vma=False,
    )
```

```python
import jax
import jax.numpy as jnp
from jax import lax
from jax.experimental import pallas as pl
from jax.experimental.pallas import tpu as pltpu
from jax.sharding import PartitionSpec as P

HEAD_DIM = 64
SEQ_MAX = 1024
EPSILON = 1e-12
ROWS = ("dp", "row")
ALL = ("dp", "row", "col")
OWNERS = ("col", "dp", "row")
BF = jnp.bfloat16
F32 = jnp.float32
LOG2E = 1.4426950408889634
SCALE = HEAD_DIM ** (-0.5)
QBLOCK = 256
EXTRA = 16


def dot_nn(a, b):
    return lax.dot_general(a, b, (((1,), (0,)), ((), ())), preferred_element_type=F32)


def dot_tn(a, b):
    return lax.dot_general(a, b, (((0,), (0,)), ((), ())), preferred_element_type=F32)


def dot_nt(a, b):
    return lax.dot_general(a, b, (((1,), (1,)), ((), ())), preferred_element_type=F32)


def mean_rows(v):
    return jnp.mean(v, axis=0, keepdims=True)


def norm_forward(values, gain, shift):
    centred = values - mean_rows(values)
    inverse = lax.rsqrt(mean_rows(centred * centred) + EPSILON)
    scaled = centred * inverse
    return scaled * gain[:, None] + shift[:, None], scaled, inverse


def norm_backward(upstream, scaled, inverse, gain):
    weighted = upstream * gain[:, None]
    return inverse * (weighted - mean_rows(weighted) - scaled * mean_rows(weighted * scaled))


def stack_rows(rows, width):
    place = lax.broadcasted_iota(jnp.int32, (EXTRA, width), 0)
    out = jnp.zeros((EXTRA, width), F32)
    for i, row in enumerate(rows):
        out = jnp.where(place == i, row, out)
    return out.astype(BF)


def three_parts(row):
    high = row.astype(BF).astype(F32)
    middle = (row - high).astype(BF).astype(F32)
    return high, middle, row - high - middle


def attend_forward_kernel(q_ref, k_ref, v_ref, mask_ref, out_ref, total_ref):
    seq = q_ref.shape[-1]
    one = jnp.ones((1, seq), F32)
    keys = jnp.concatenate([k_ref[0, 0, 0], stack_rows([mask_ref[...]], seq)], axis=0).T
    queries = jnp.concatenate([q_ref[0, 0, 0], stack_rows([one], seq)], axis=0)
    values = v_ref[0, 0, 0]
    for j in range(seq // QBLOCK):
        cols = slice(j * QBLOCK, (j + 1) * QBLOCK)
        scores = dot_nn(keys, queries[:, cols])
        largest = jnp.max(scores, axis=0, keepdims=True)
        exponent = jnp.exp2((scores - largest) * (SCALE * LOG2E))
        total = jnp.sum(exponent, axis=0, keepdims=True)
        weights = (exponent * (1.0 / total)).astype(BF)
        out_ref[0, :, cols] = dot_nn(values, weights).astype(BF)
        total_ref[0, :, cols] = largest + jnp.log(total) * (1.0 / SCALE)


def attend_backward_kernel(
    q_ref, k_ref, v_ref, mask_ref, out_ref, total_ref, up_ref,
    grad_qk_ref, grad_v_ref, bias_ref, dk_ref, dv_ref,
):
    seq = q_ref.shape[-1]
    one = jnp.ones((1, seq), F32)
    keys = k_ref[0, 0, 0]
    queries = q_ref[0, 0, 0]
    up = up_ref[0]
    delta = jnp.sum(up.astype(F32) * out_ref[0].astype(F32), axis=0, keepdims=True)
    key_side = jnp.concatenate([keys, stack_rows([mask_ref[...], one, one, one], seq)], axis=0).T
    value_side = jnp.concatenate([v_ref[0, 0, 0], stack_rows([one, one, one], seq)], axis=0).T
    query_side = jnp.concatenate([queries, stack_rows([one, *three_parts(-total_ref[0])], seq)], axis=0)
    up_side = jnp.concatenate([up, stack_rows(three_parts(-delta), seq)], axis=0)
    lanes = 128
    sum_q = jnp.zeros((HEAD_DIM, lanes), F32)
    for j in range(seq // QBLOCK):
        cols = slice(j * QBLOCK, (j + 1) * QBLOCK)
        weights = jnp.exp2(dot_nn(key_side, query_side[:, cols]) * (SCALE * LOG2E))
        d_scores = (weights * dot_nn(value_side, up_side[:, cols])).astype(BF)
        d_q = dot_nn(keys, d_scores) * SCALE
        for part in range(QBLOCK // lanes):
            sum_q += d_q[:, part * lanes : (part + 1) * lanes]
        grad_qk_ref[0, 0, 0, :, cols] = d_q.astype(BF)
        d_k = dot_nt(queries[:, cols], d_scores)
        d_v = dot_nt(up[:, cols], weights.astype(BF))
        if j == 0:
            dk_ref[...] = d_k
            dv_ref[...] = d_v
        else:
            dk_ref[...] += d_k
            dv_ref[...] += d_v
    grad_qk_ref[0, 1, 0] = (dk_ref[...] * SCALE).astype(BF)
    grad_v_ref[0, 0, 0] = dv_ref[...].astype(BF)
    bias_ref[0, 0] = sum_q
    sum_v = jnp.zeros((HEAD_DIM, lanes), F32)
    for part in range(seq // lanes):
        sum_v += dv_ref[:, part * lanes : (part + 1) * lanes]
    bias_ref[0, 1] = sum_v


def projection_spec(first, count, per_col, seq):
    return pl.BlockSpec((1, count, 1, HEAD_DIM, seq), lambda h: (h // per_col, first, h % per_col, 0, 0))


def head_spec(rows, seq):
    return pl.BlockSpec((1, rows, seq), lambda h: (h, 0, 0))


def qkv_specs(per_col, seq):
    return [
        projection_spec(0, 1, per_col, seq), projection_spec(1, 1, per_col, seq), projection_spec(0, 1, per_col, seq),
        pl.BlockSpec((1, seq), lambda h: (0, 0)),
    ]


def attend_forward(qk, v, mask):
    cols, _, per_col, _, seq = qk.shape
    heads = cols * per_col
    return pl.pallas_call(
        attend_forward_kernel,
        grid=(heads,),
        in_specs=qkv_specs(per_col, seq),
        out_specs=[head_spec(HEAD_DIM, seq), head_spec(1, seq)],
        out_shape=[
            jax.ShapeDtypeStruct((heads, HEAD_DIM, seq), BF),
            jax.ShapeDtypeStruct((heads, 1, seq), F32),
        ],
        cost_estimate=pl.CostEstimate(
            flops=heads * seq * seq * HEAD_DIM * 16, bytes_accessed=heads * seq * HEAD_DIM * 8,
            transcendentals=heads * seq * seq,
        ),
        name="attend_forward",
    )(qk, qk, v, mask)


def attend_backward(qk, v, mask, attended, total, d_attended):
    cols, _, per_col, _, seq = qk.shape
    heads = cols * per_col
    return pl.pallas_call(
        attend_backward_kernel,
        grid=(heads,),
        in_specs=qkv_specs(per_col, seq)
        + [head_spec(HEAD_DIM, seq), head_spec(1, seq), head_spec(HEAD_DIM, seq)],
        out_specs=[
            projection_spec(0, 2, per_col, seq),
            projection_spec(0, 1, per_col, seq),
            pl.BlockSpec((1, 2, HEAD_DIM, 128), lambda h: (h, 0, 0, 0)),
        ],
        out_shape=[
            jax.ShapeDtypeStruct(qk.shape, BF),
            jax.ShapeDtypeStruct(v.shape, BF),
            jax.ShapeDtypeStruct((heads, 2, HEAD_DIM, 128), F32),
        ],
        scratch_shapes=[pltpu.VMEM((HEAD_DIM, seq), F32), pltpu.VMEM((HEAD_DIM, seq), F32)],
        cost_estimate=pl.CostEstimate(
            flops=heads * seq * seq * HEAD_DIM * 40, bytes_accessed=heads * seq * HEAD_DIM * 16,
            transcendentals=heads * seq * seq,
        ),
        name="attend_backward",
    )(qk, qk, v, mask, attended, total, d_attended)


def axis_bits(name):
    size = lax.axis_size(name)
    return [(name, 1 << b) for b in reversed(range(size.bit_length() - 1))]


def swap(a, name, bit):
    return lax.ppermute(a, name, [(i, i ^ bit) for i in range(lax.axis_size(name))])


def my_bit(name, bit):
    return (lax.axis_index(name) // bit) % 2


def gather_blocks(shard, order):
    dims = axis_bits("col") + axis_bits("dp") + axis_bits("row")
    a = shard.reshape((1,) * len(dims) + shard.shape)
    for name, bit in order:
        dim = dims.index((name, bit))
        other = swap(a, name, bit)
        high = my_bit(name, bit) == 1
        a = jnp.concatenate([jnp.where(high, other, a), jnp.where(high, a, other)], axis=dim)
    return a.reshape(lax.axis_size("col"), -1, shard.shape[1])


def scatter_blocks(grad, order):
    dims = axis_bits("col") + axis_bits("dp") + axis_bits("row")
    rows = grad.shape[0] * grad.shape[1] >> len(dims)
    a = grad.astype(BF).reshape((2,) * len(dims) + (rows, grad.shape[2]))
    for name, bit in order:
        dim = dims.index((name, bit))
        mine = my_bit(name, bit)
        other = swap(lax.dynamic_index_in_dim(a, 1 - mine, dim), name, bit)
        a = lax.dynamic_index_in_dim(a, mine, dim).astype(F32) + other.astype(F32)
        a = a.astype(BF)
    return a.reshape(rows, grad.shape[2]).astype(F32)


def spread_windows(a):
    cols = lax.axis_size("col")
    col = lax.axis_index("col")
    rows, seq = a.shape[0] // cols, a.shape[1]
    parts = [lax.dynamic_slice_in_dim(a, col * rows, rows, axis=0)]
    for step in range(1, cols):
        block = lax.dynamic_slice_in_dim(a, (col ^ step) * rows, rows, axis=0)
        parts.append(lax.ppermute(block, "col", [(i, i ^ step) for i in range(cols)]))
    out = jnp.zeros((rows, cols * seq), F32)
    for step, part in enumerate(parts):
        out = lax.dynamic_update_slice_in_dim(out, part.astype(F32), (col ^ step) * seq, axis=1)
    return out


def local(
    tokens, w_qkv, bias_qv, w_attn_out, bias_attn_out, w_in, bias_in, w_out, bias_out,
    norm_gains, norm_biases, seq_lengths, seq_offsets, cotangent,
):
    cols = lax.axis_size("col")
    col = lax.axis_index("col")
    rows, _, width = w_qkv.shape
    groups = lax.axis_size("dp") * lax.axis_size("row")
    d = rows * groups
    heads = d // HEAD_DIM
    hid = w_in.shape[1]

    col_bits, row_bits, dp_bits = axis_bits("col"), axis_bits("row"), axis_bits("dp")
    near_first = col_bits[::-1] + row_bits[::-1] + dp_bits
    far_first = col_bits[::-1] + row_bits + dp_bits

    def gather(shard):
        return lax.all_gather(shard, OWNERS, axis=0, tiled=True).reshape(cols, d, shard.shape[1])

    w_flat = w_qkv.reshape(rows, 3 * width)
    full_qk = gather_blocks(w_flat[:, : 2 * width], near_first)
    full_vo = gather_blocks(jnp.concatenate([w_flat[:, 2 * width :], w_attn_out], axis=1), far_first)
    full_in = gather(w_in)
    full_out = gather(w_out)
    full_v = full_vo[:, :, :width]
    full_attn = full_vo[:, :, width:]

    vectors = jnp.concatenate(
        [bias_qv, bias_attn_out[None], bias_out[None], norm_gains, norm_biases, bias_in.reshape(-1, width)], axis=0
    )
    vectors = vectors.reshape((1,) * len(col_bits) + vectors.shape)
    for dim, (name, bit) in enumerate(col_bits):
        other = swap(vectors, name, bit)
        high = my_bit(name, bit) == 1
        vectors = jnp.concatenate([jnp.where(high, other, vectors), jnp.where(high, vectors, other)], axis=dim)
    vectors = vectors.reshape(cols, -1, width)
    bias_q, bias_v = vectors[:, 0], vectors[:, 1]
    bias_attn_out, bias_out = vectors[:, 2].reshape(d), vectors[:, 3].reshape(d)
    gains = [vectors[:, 4].reshape(d), vectors[:, 5].reshape(d)]
    shifts = [vectors[:, 6].reshape(d), vectors[:, 7].reshape(d)]
    bias_in = vectors[:, 8:].reshape(cols, hid)

    def to_window(a):
        return lax.all_to_all(a, "col", split_axis=1, concat_axis=0, tiled=True)

    x = to_window(tokens)
    up = to_window(cotangent)
    length = lax.dynamic_index_in_dim(seq_lengths, col, keepdims=False)
    offset = lax.dynamic_index_in_dim(seq_offsets, col, keepdims=False)
    places = lax.broadcasted_iota(jnp.int32, (1, SEQ_MAX), 1)
    live_mask = (places >= offset) & (places < offset + length)
    live = live_mask.astype(F32)
    key_mask = jnp.where(live_mask, 0.0, -1e30).astype(F32)

    def project(weights, shift):
        out = jnp.einsum("cdn,dt->cnt", weights, x, preferred_element_type=F32) + shift[:, :, None]
        return out.astype(BF).reshape(cols, -1, width // HEAD_DIM, HEAD_DIM, SEQ_MAX)

    qk = project(full_qk, jnp.concatenate([bias_q, jnp.zeros_like(bias_q)], axis=1))
    values = project(full_v, bias_v)
    attended, total = attend_forward(qk, values, key_mask)
    attended_cols = attended.reshape(cols, width, SEQ_MAX)
    first_sum = (
        x.astype(F32) + jnp.einsum("cde,cet->dt", full_attn, attended_cols, preferred_element_type=F32)
        + bias_attn_out[:, None]
    )
    normed, xhat1, rstd1 = norm_forward(first_sum, gains[0], shifts[0])
    normed_low = normed.astype(BF)
    hidden = jnp.einsum("cdf,dt->cft", full_in, normed_low, preferred_element_type=F32) + bias_in[:, :, None]
    cdf = 0.5 * (1.0 + lax.erf(hidden * 0.5**0.5))
    active = (hidden * cdf).astype(BF)
    slope = cdf + hidden * jnp.exp(-0.5 * hidden * hidden) * 0.3989422804014327
    second_sum = (
        normed + jnp.einsum("cdf,cft->dt", full_out, active, preferred_element_type=F32) + bias_out[:, None]
    )
    result, xhat2, rstd2 = norm_forward(second_sum, gains[1], shifts[1])
    activations = spread_windows((result * live).astype(BF))

    upstream = up.astype(F32) * live
    gain_two = jnp.sum(upstream * xhat2, axis=1)
    shift_two = jnp.sum(upstream, axis=1)
    d_second = norm_backward(upstream, xhat2, rstd2, gains[1])
    g_bias_out = jnp.sum(d_second, axis=1)
    d_second_low = d_second.astype(BF)
    g_out = jnp.einsum("dt,cft->cdf", d_second_low, active, preferred_element_type=F32)
    g_out = scatter_blocks(g_out, dp_bits + row_bits + col_bits)
    d_hidden = jnp.einsum("cdf,dt->cft", full_out, d_second_low, preferred_element_type=F32) * slope
    g_bias_in = jnp.sum(d_hidden, axis=2)
    d_hidden_low = d_hidden.astype(BF)
    g_in = jnp.einsum("dt,cft->cdf", normed_low, d_hidden_low, preferred_element_type=F32)
    g_in = scatter_blocks(g_in, dp_bits + row_bits[::-1] + col_bits)
    d_normed = d_second + jnp.einsum("cdf,cft->dt", full_in, d_hidden_low, preferred_element_type=F32)
    gain_one = jnp.sum(d_normed * xhat1, axis=1)
    shift_one = jnp.sum(d_normed, axis=1)
    d_first = norm_backward(d_normed, xhat1, rstd1, gains[0])
    g_bias_attn = jnp.sum(d_first, axis=1)
    d_first_low = d_first.astype(BF)
    d_attended = jnp.einsum("cde,dt->cet", full_attn, d_first_low, preferred_element_type=F32).astype(BF)
    d_attended = d_attended.reshape(heads, HEAD_DIM, SEQ_MAX)
    g_attn = jnp.einsum("dt,cet->cde", d_first_low, attended_cols, preferred_element_type=F32)
    g_attn = scatter_blocks(g_attn, dp_bits + row_bits + col_bits)
    d_qk, d_v, bias_sums = attend_backward(qk, values, key_mask, attended, total, d_attended)
    d_qk = d_qk.reshape(cols, 2 * width, SEQ_MAX)
    d_v = d_v.reshape(cols, width, SEQ_MAX)
    bias_sums = jnp.sum(bias_sums, axis=3)
    g_bias_q, g_bias_v = bias_sums[:, 0].reshape(d), bias_sums[:, 1].reshape(d)
    g_qk = jnp.einsum("dt,cnt->cdn", x, d_qk, preferred_element_type=F32)
    g_qk = scatter_blocks(g_qk, dp_bits + row_bits[::-1] + col_bits)
    g_v = jnp.einsum("dt,cnt->cdn", x, d_v, preferred_element_type=F32)
    g_v = scatter_blocks(g_v, dp_bits + row_bits + col_bits)
    token_grad = (
        d_first + jnp.einsum("cdn,cnt->dt", full_qk, d_qk, preferred_element_type=F32)
        + jnp.einsum("cdn,cnt->dt", full_v, d_v, preferred_element_type=F32)
    )
    token_grad = spread_windows(token_grad.astype(BF))

    small = jnp.stack([g_bias_q, g_bias_v, g_bias_attn, g_bias_out, gain_one, gain_two, shift_one, shift_two])
    small = small.reshape(8, cols, width).transpose(1, 0, 2)
    small = jnp.concatenate([small, g_bias_in.reshape(cols, -1, width)], axis=1)
    small = small.reshape((2,) * len(col_bits) + small.shape[1:])
    for dim, (name, bit) in enumerate(col_bits):
        mine = my_bit(name, bit)
        other = swap(lax.dynamic_index_in_dim(small, 1 - mine, dim), name, bit)
        small = lax.dynamic_index_in_dim(small, mine, dim) + other
    own = small.reshape(small.shape[-2:])
    for name, bit in row_bits + dp_bits:
        own = own + swap(own, name, bit)
    return (
        activations, token_grad, jnp.concatenate([g_qk, g_v], axis=1).reshape(rows, 3, width), own[0:2],
        g_attn, own[2], g_in, own[8:].reshape(hid), g_out, own[3], own[4:6], own[6:8],
    )


def solution(mesh):
    return jax.shard_map(
        local,
        mesh=mesh,
        in_specs=(
            P("col", ROWS), P(ROWS, None, "col"), P(None, "col"), P(ROWS, "col"), P("col"),
            P(ROWS, "col"), P("col"), P(ROWS, "col"), P("col"), P(None, "col"), P(None, "col"),
            P(ROWS), P(ROWS), P("col", ROWS),
        ),
        out_specs=(
            P("col", ROWS), P("col", ROWS), P(ROWS, None, "col"), P(None, "col"), P(ROWS, "col"),
            P("col"), P(ROWS, "col"), P("col"), P(ROWS, "col"), P("col"), P(None, "col"), P(None, "col"),
        ),
        check_vma=False,
    )
```

```python
import jax
import jax.numpy as jnp
from jax import lax
from jax.experimental import pallas as pl
from jax.experimental.pallas import tpu as pltpu
from jax.sharding import PartitionSpec as P

HEAD_DIM = 64
SEQ_MAX = 1024
EPSILON = 1e-12
ROWS = ("dp", "row")
ALL = ("dp", "row", "col")
OWNERS = ("col", "dp", "row")
BF = jnp.bfloat16
F32 = jnp.float32
LOG2E = 1.4426950408889634
SCALE = HEAD_DIM ** (-0.5)
QBLOCK = 256
EXTRA = 16


def dot_nn(a, b):
    return lax.dot_general(a, b, (((1,), (0,)), ((), ())), preferred_element_type=F32)


def dot_tn(a, b):
    return lax.dot_general(a, b, (((0,), (0,)), ((), ())), preferred_element_type=F32)


def dot_nt(a, b):
    return lax.dot_general(a, b, (((1,), (1,)), ((), ())), preferred_element_type=F32)


def mean_rows(v):
    return jnp.mean(v, axis=0, keepdims=True)


def norm_forward(values, gain, shift):
    centred = values - mean_rows(values)
    inverse = lax.rsqrt(mean_rows(centred * centred) + EPSILON)
    scaled = centred * inverse
    return scaled * gain[:, None] + shift[:, None], scaled, inverse


def norm_backward(upstream, scaled, inverse, gain):
    weighted = upstream * gain[:, None]
    return inverse * (weighted - mean_rows(weighted) - scaled * mean_rows(weighted * scaled))


def stack_rows(rows, width):
    place = lax.broadcasted_iota(jnp.int32, (EXTRA, width), 0)
    out = jnp.zeros((EXTRA, width), F32)
    for i, row in enumerate(rows):
        out = jnp.where(place == i, row, out)
    return out.astype(BF)


def three_parts(row):
    high = row.astype(BF).astype(F32)
    middle = (row - high).astype(BF).astype(F32)
    return high, middle, row - high - middle


def attend_forward_kernel(q_ref, k_ref, v_ref, mask_ref, out_ref, total_ref):
    seq = q_ref.shape[-1]
    one = jnp.ones((1, seq), F32)
    keys = jnp.concatenate([k_ref[0, 0, 0], stack_rows([mask_ref[...]], seq)], axis=0).T
    queries = jnp.concatenate([q_ref[0, 0, 0], stack_rows([one], seq)], axis=0)
    values = v_ref[0, 0, 0]
    for j in range(seq // QBLOCK):
        cols = slice(j * QBLOCK, (j + 1) * QBLOCK)
        scores = dot_nn(keys, queries[:, cols])
        largest = jnp.max(scores, axis=0, keepdims=True)
        exponent = jnp.exp2((scores - largest) * (SCALE * LOG2E))
        total = jnp.sum(exponent, axis=0, keepdims=True)
        weights = (exponent * (1.0 / total)).astype(BF)
        out_ref[0, :, cols] = dot_nn(values, weights).astype(BF)
        total_ref[0, :, cols] = largest + jnp.log(total) * (1.0 / SCALE)


def attend_backward_kernel(
    q_ref, k_ref, v_ref, mask_ref, out_ref, total_ref, up_ref,
    grad_qk_ref, grad_v_ref, bias_ref, dk_ref, dv_ref,
):
    seq = q_ref.shape[-1]
    one = jnp.ones((1, seq), F32)
    keys = k_ref[0, 0, 0]
    queries = q_ref[0, 0, 0]
    up = up_ref[0]
    delta = jnp.sum(up.astype(F32) * out_ref[0].astype(F32), axis=0, keepdims=True)
    key_side = jnp.concatenate([keys, stack_rows([mask_ref[...], one, one, one], seq)], axis=0).T
    value_side = jnp.concatenate([v_ref[0, 0, 0], stack_rows([one, one, one], seq)], axis=0).T
    query_side = jnp.concatenate([queries, stack_rows([one, *three_parts(-total_ref[0])], seq)], axis=0)
    up_side = jnp.concatenate([up, stack_rows(three_parts(-delta), seq)], axis=0)
    lanes = 128
    sum_q = jnp.zeros((HEAD_DIM, lanes), F32)
    for j in range(seq // QBLOCK):
        cols = slice(j * QBLOCK, (j + 1) * QBLOCK)
        weights = jnp.exp2(dot_nn(key_side, query_side[:, cols]) * (SCALE * LOG2E))
        d_scores = (weights * dot_nn(value_side, up_side[:, cols])).astype(BF)
        d_q = dot_nn(keys, d_scores) * SCALE
        for part in range(QBLOCK // lanes):
            sum_q += d_q[:, part * lanes : (part + 1) * lanes]
        grad_qk_ref[0, 0, 0, :, cols] = d_q.astype(BF)
        d_k = dot_nt(queries[:, cols], d_scores)
        d_v = dot_nt(up[:, cols], weights.astype(BF))
        if j == 0:
            dk_ref[...] = d_k
            dv_ref[...] = d_v
        else:
            dk_ref[...] += d_k
            dv_ref[...] += d_v
    grad_qk_ref[0, 1, 0] = (dk_ref[...] * SCALE).astype(BF)
    grad_v_ref[0, 0, 0] = dv_ref[...].astype(BF)
    bias_ref[0, 0] = sum_q
    sum_v = jnp.zeros((HEAD_DIM, lanes), F32)
    for part in range(seq // lanes):
        sum_v += dv_ref[:, part * lanes : (part + 1) * lanes]
    bias_ref[0, 1] = sum_v


def projection_spec(first, count, per_col, seq):
    return pl.BlockSpec((1, count, 1, HEAD_DIM, seq), lambda h: (h // per_col, first, h % per_col, 0, 0))


def head_spec(rows, seq):
    return pl.BlockSpec((1, rows, seq), lambda h: (h, 0, 0))


def qkv_specs(per_col, seq):
    return [
        projection_spec(0, 1, per_col, seq), projection_spec(1, 1, per_col, seq), projection_spec(0, 1, per_col, seq),
        pl.BlockSpec((1, seq), lambda h: (0, 0)),
    ]


def attend_forward(qk, v, mask):
    cols, _, per_col, _, seq = qk.shape
    heads = cols * per_col
    return pl.pallas_call(
        attend_forward_kernel,
        grid=(heads,),
        in_specs=qkv_specs(per_col, seq),
        out_specs=[head_spec(HEAD_DIM, seq), head_spec(1, seq)],
        out_shape=[
            jax.ShapeDtypeStruct((heads, HEAD_DIM, seq), BF),
            jax.ShapeDtypeStruct((heads, 1, seq), F32),
        ],
        cost_estimate=pl.CostEstimate(
            flops=heads * seq * seq * HEAD_DIM * 16, bytes_accessed=heads * seq * HEAD_DIM * 8,
            transcendentals=heads * seq * seq,
        ),
        name="attend_forward",
    )(qk, qk, v, mask)


def attend_backward(qk, v, mask, attended, total, d_attended):
    cols, _, per_col, _, seq = qk.shape
    heads = cols * per_col
    return pl.pallas_call(
        attend_backward_kernel,
        grid=(heads,),
        in_specs=qkv_specs(per_col, seq)
        + [head_spec(HEAD_DIM, seq), head_spec(1, seq), head_spec(HEAD_DIM, seq)],
        out_specs=[
            projection_spec(0, 2, per_col, seq),
            projection_spec(0, 1, per_col, seq),
            pl.BlockSpec((1, 2, HEAD_DIM, 128), lambda h: (h, 0, 0, 0)),
        ],
        out_shape=[
            jax.ShapeDtypeStruct(qk.shape, BF),
            jax.ShapeDtypeStruct(v.shape, BF),
            jax.ShapeDtypeStruct((heads, 2, HEAD_DIM, 128), F32),
        ],
        scratch_shapes=[pltpu.VMEM((HEAD_DIM, seq), F32), pltpu.VMEM((HEAD_DIM, seq), F32)],
        cost_estimate=pl.CostEstimate(
            flops=heads * seq * seq * HEAD_DIM * 40, bytes_accessed=heads * seq * HEAD_DIM * 16,
            transcendentals=heads * seq * seq,
        ),
        name="attend_backward",
    )(qk, qk, v, mask, attended, total, d_attended)


def axis_bits(name):
    size = lax.axis_size(name)
    return [(name, 1 << b) for b in reversed(range(size.bit_length() - 1))]


def my_bit(name, bit):
    return (lax.axis_index(name) // bit) % 2


def partner(name, bit):
    return {name: lax.axis_index(name) + bit * (1 - 2 * my_bit(name, bit))}


def all_bits():
    return axis_bits("col") + axis_bits("dp") + axis_bits("row")


def col_peer(step):
    cols = lax.axis_size("col")
    col = lax.axis_index("col")
    return (col + step) % cols, (col + cols - step) % cols


def remote(src, dst, send, recv, device):
    return pltpu.make_async_remote_copy(
        src_ref=src, dst_ref=dst, send_sem=send, recv_sem=recv, device_id=device,
        device_id_type=pl.DeviceIdType.MESH,
    )


def meet_partners():
    barrier = pltpu.get_barrier_semaphore()
    devices = [partner(name, bit) for name, bit in axis_bits("dp") + axis_bits("row")]
    devices += [{"col": col_peer(step)[0]} for step in range(1, lax.axis_size("col"))]
    for device in devices:
        pl.semaphore_signal(barrier, inc=1, device_id=device, device_id_type=pl.DeviceIdType.MESH)
    pl.semaphore_wait(barrier, len(devices))


def head_kernel(
    orders, qk_ref, vo_ref, tokens_ref, vectors_ref, full_qk_ref, full_vo_ref, x_ref, all_vectors_ref,
    own_sem, block_send, block_recv, col_send, col_recv,
):
    dims = all_bits()
    cols, col = lax.axis_size("col"), lax.axis_index("col")
    feats, seq = tokens_ref.shape[0], x_ref.shape[1]
    place = [my_bit(name, bit) for name, bit in dims]
    pieces = [(qk_ref, full_qk_ref), (vo_ref, full_vo_ref)]
    my_feats = pl.ds(pl.multiple_of(col * feats, 8), feats)
    own = [pltpu.make_async_copy(src, dst.at[tuple(place)], own_sem.at[i]) for i, (src, dst) in enumerate(pieces)]
    own.append(
        pltpu.make_async_copy(
            tokens_ref.at[:, pl.ds(pl.multiple_of(col * seq, 128), seq)], x_ref.at[my_feats], own_sem.at[2]
        )
    )
    own.append(pltpu.make_async_copy(vectors_ref, all_vectors_ref.at[col], own_sem.at[3]))
    for copy in own:
        copy.start()
    meet_partners()

    def stage(piece, step):
        src, full = pieces[piece]
        done = orders[piece][:step]
        index = tuple(slice(None) if bit in done else at for bit, at in zip(dims, place))
        return remote(
            src if step == 0 else full.at[index], full.at[index], block_send.at[piece, step],
            block_recv.at[piece, step], partner(*orders[piece][step]),
        )

    stages = [[stage(piece, step) for step in range(len(dims))] for piece in range(2)]
    for piece in range(2):
        stages[piece][0].start()
    transposes = []
    for step in range(1, cols):
        to, _ = col_peer(step)
        transposes.append(
            remote(vectors_ref, all_vectors_ref.at[col], col_send.at[0, step], col_recv.at[0, step], {"col": to})
        )
        transposes.append(
            remote(
                tokens_ref.at[:, pl.ds(pl.multiple_of(to * seq, 128), seq)], x_ref.at[my_feats],
                col_send.at[1, step], col_recv.at[1, step], {"col": to},
            )
        )
    for copy in transposes:
        copy.start()
    for copy in own:
        copy.wait()
    for step in range(len(dims)):
        for piece in range(2):
            stages[piece][step].wait()
            if step + 1 < len(dims):
                stages[piece][step + 1].start()
    for copy in transposes:
        copy.wait()


def head(orders, qk, vo, tokens, vectors):
    dims = all_bits()
    cols = lax.axis_size("col")
    twos = (2,) * len(dims)
    vmem = pl.BlockSpec(memory_space=pltpu.VMEM)
    return pl.pallas_call(
        lambda *refs: head_kernel(orders, *refs),
        in_specs=[vmem] * 4,
        out_specs=[vmem] * 4,
        out_shape=[
            jax.ShapeDtypeStruct(twos + qk.shape, BF),
            jax.ShapeDtypeStruct(twos + vo.shape, BF),
            jax.ShapeDtypeStruct((cols * tokens.shape[0], SEQ_MAX), BF),
            jax.ShapeDtypeStruct((cols,) + vectors.shape, F32),
        ],
        scratch_shapes=[
            pltpu.SemaphoreType.DMA((4,)),
            pltpu.SemaphoreType.DMA((2, len(dims))), pltpu.SemaphoreType.DMA((2, len(dims))),
            pltpu.SemaphoreType.DMA((2, cols)), pltpu.SemaphoreType.DMA((2, cols)),
        ],
        compiler_params=pltpu.CompilerParams(collective_id=0, has_side_effects=True),
        name="head",
    )(qk, vo, tokens, vectors)


def tail_kernel(orders, *refs):
    dims = all_bits()
    levels = len(dims)
    count = len(orders)
    cols, col = lax.axis_size("col"), lax.axis_index("col")
    grads, (token_ref, small_ref) = refs[:count], refs[count : count + 2]
    refs = refs[count + 2 :]
    sums, (out_ref, own_ref) = refs[:count], refs[count : count + 2]
    refs = refs[count + 2 :]
    landed = [refs[i * levels : (i + 1) * levels] for i in range(count)]
    refs = refs[count * levels :]
    (
        token_landed, small_landed, small_sum, block_send, block_recv, col_send, col_recv, small_send, small_recv,
    ) = refs
    feats, seq = token_landed.shape[1], token_landed.shape[2]
    small_bits = axis_bits("row") + axis_bits("dp")
    meet_partners()

    def views(piece, step):
        left = [bit for bit in dims if bit not in orders[piece][:step]]
        axis = left.index(orders[piece][step])
        return grads[piece] if step == 0 else landed[piece][step - 1], axis, my_bit(*orders[piece][step])

    def stage(piece, step):
        operand, axis, mine = views(piece, step)
        return remote(
            operand.at[(slice(None),) * axis + (1 - mine,)], landed[piece][step], block_send.at[piece, step],
            block_recv.at[piece, step], partner(*orders[piece][step]),
        )

    def add(piece, step):
        operand, axis, mine = views(piece, step)
        arrived = landed[piece][step]
        free = levels - 1 - step

        def body(i, carry):
            index = [(i // 2 ** (free - 1 - k)) % 2 for k in range(free)]
            kept = operand[tuple(index[:axis] + [mine] + index[axis:])].astype(F32)
            total = kept + arrived[tuple(index)].astype(F32)
            if free:
                arrived[tuple(index)] = total.astype(BF)
            else:
                sums[piece][...] = total
            return carry

        if free:
            lax.fori_loop(0, 2**free, body, 0)
        else:
            body(0, 0)

    stages = [[stage(piece, step) for step in range(levels)] for piece in range(count)]
    for piece in range(count):
        stages[piece][0].start()
    small_copies = []
    token_copies = []
    for step in range(1, cols):
        to, _ = col_peer(step)
        small_copies.append(
            remote(small_ref.at[to], small_landed.at[step], col_send.at[0, step], col_recv.at[0, step], {"col": to})
        )
        token_copies.append(
            remote(
                token_ref.at[pl.ds(pl.multiple_of(to * feats, 8), feats)], token_landed.at[step],
                col_send.at[1, step], col_recv.at[1, step], {"col": to},
            )
        )
    for copy in small_copies + token_copies:
        copy.start()
    out_ref[:, pl.ds(pl.multiple_of(col * seq, 128), seq)] = token_ref[
        pl.ds(pl.multiple_of(col * feats, 8), feats)
    ].astype(F32)
    for copy in small_copies:
        copy.wait()
    total = small_ref[col]
    for step in range(1, cols):
        total = total + small_landed[step]
    small_sum[0] = total
    for step in range(max(levels, len(small_bits))):
        if step < len(small_bits):
            small_copy = remote(
                small_sum.at[step], small_landed.at[cols + step], small_send.at[step], small_recv.at[step],
                partner(*small_bits[step]),
            )
            small_copy.start()
        for piece in range(count):
            if step < levels:
                stages[piece][step].wait()
                add(piece, step)
                if step + 1 < levels:
                    stages[piece][step + 1].start()
        if step < len(small_bits):
            small_copy.wait()
            small_sum[step + 1] = small_sum[step] + small_landed[cols + step]
    own_ref[...] = small_sum[len(small_bits)]
    for step in range(1, cols):
        _, source = col_peer(step)
        token_copies[step - 1].wait()
        out_ref[:, pl.ds(pl.multiple_of(source * seq, 128), seq)] = token_landed[step].astype(F32)


def tail(orders, grads, token_grad, small):
    dims = all_bits()
    levels = len(dims)
    cols = lax.axis_size("col")
    rows = grads[0].shape[0] * grads[0].shape[1] >> levels
    feats = token_grad.shape[0] // cols
    grads = [g.reshape((2,) * levels + (rows, g.shape[2])) for g in grads]
    widths = [g.shape[-1] for g in grads]
    small_bits = axis_bits("row") + axis_bits("dp")
    vmem = pl.BlockSpec(memory_space=pltpu.VMEM)
    dma = pltpu.SemaphoreType.DMA
    return pl.pallas_call(
        lambda *refs: tail_kernel(orders, *refs),
        in_specs=[vmem] * (len(grads) + 2),
        out_specs=[vmem] * (len(grads) + 2),
        out_shape=[jax.ShapeDtypeStruct((rows, w), F32) for w in widths]
        + [jax.ShapeDtypeStruct((feats, cols * SEQ_MAX), F32), jax.ShapeDtypeStruct(small.shape[1:], F32)],
        scratch_shapes=[
            pltpu.VMEM((2,) * (levels - 1 - step) + (rows, w), BF) for w in widths for step in range(levels)
        ]
        + [
            pltpu.VMEM((cols, feats, SEQ_MAX), BF),
            pltpu.VMEM((cols + len(small_bits),) + small.shape[1:], F32),
            pltpu.VMEM((len(small_bits) + 1,) + small.shape[1:], F32),
            dma((len(grads), levels)), dma((len(grads), levels)), dma((2, cols)), dma((2, cols)),
            dma((len(small_bits),)), dma((len(small_bits),)),
        ],
        compiler_params=pltpu.CompilerParams(collective_id=1, has_side_effects=True),
        name="tail",
    )(*grads, token_grad, small)


def local(
    tokens, w_qkv, bias_qv, w_attn_out, bias_attn_out, w_in, bias_in, w_out, bias_out,
    norm_gains, norm_biases, seq_lengths, seq_offsets, cotangent,
):
    cols = lax.axis_size("col")
    col = lax.axis_index("col")
    rows, _, width = w_qkv.shape
    groups = lax.axis_size("dp") * lax.axis_size("row")
    d = rows * groups
    heads = d // HEAD_DIM
    hid = w_in.shape[1]

    col_bits, row_bits, dp_bits = axis_bits("col"), axis_bits("row"), axis_bits("dp")
    near_first = col_bits[::-1] + row_bits[::-1] + dp_bits
    far_first = col_bits[::-1] + row_bits + dp_bits

    def gather(shard):
        return lax.all_gather(shard, OWNERS, axis=0, tiled=True).reshape(cols, d, shard.shape[1])

    full_in = gather(w_in)
    full_out = gather(w_out)
    vectors = jnp.concatenate(
        [bias_qv, bias_attn_out[None], bias_out[None], norm_gains, norm_biases, bias_in.reshape(-1, width)], axis=0
    )
    w_flat = w_qkv.reshape(rows, 3 * width)
    w_vo = jnp.concatenate([w_flat[:, 2 * width :], w_attn_out], axis=1)
    full_qk, full_vo, x, vectors = head((near_first, far_first), w_flat[:, : 2 * width], w_vo, tokens, vectors)
    full_qk = full_qk.reshape(cols, d, 2 * width)
    full_vo = full_vo.reshape(cols, d, 2 * width)
    full_v = full_vo[:, :, :width]
    full_attn = full_vo[:, :, width:]
    bias_q, bias_v = vectors[:, 0], vectors[:, 1]
    bias_attn_out, bias_out = vectors[:, 2].reshape(d), vectors[:, 3].reshape(d)
    gains = [vectors[:, 4].reshape(d), vectors[:, 5].reshape(d)]
    shifts = [vectors[:, 6].reshape(d), vectors[:, 7].reshape(d)]
    bias_in = vectors[:, 8:].reshape(cols, hid)

    def to_window(a):
        return lax.all_to_all(a, "col", split_axis=1, concat_axis=0, tiled=True)

    up = to_window(cotangent)
    length = lax.dynamic_index_in_dim(seq_lengths, col, keepdims=False)
    offset = lax.dynamic_index_in_dim(seq_offsets, col, keepdims=False)
    places = lax.broadcasted_iota(jnp.int32, (1, SEQ_MAX), 1)
    live_mask = (places >= offset) & (places < offset + length)
    live = live_mask.astype(F32)
    key_mask = jnp.where(live_mask, 0.0, -1e30).astype(F32)

    def project(weights, shift):
        out = jnp.einsum("cdn,dt->cnt", weights, x, preferred_element_type=F32) + shift[:, :, None]
        return out.astype(BF).reshape(cols, -1, width // HEAD_DIM, HEAD_DIM, SEQ_MAX)

    qk = project(full_qk, jnp.concatenate([bias_q, jnp.zeros_like(bias_q)], axis=1))
    values = project(full_v, bias_v)
    attended, total = attend_forward(qk, values, key_mask)
    attended_cols = attended.reshape(cols, width, SEQ_MAX)
    first_sum = (
        x.astype(F32) + jnp.einsum("cde,cet->dt", full_attn, attended_cols, preferred_element_type=F32)
        + bias_attn_out[:, None]
    )
    normed, xhat1, rstd1 = norm_forward(first_sum, gains[0], shifts[0])
    normed_low = normed.astype(BF)
    hidden = jnp.einsum("cdf,dt->cft", full_in, normed_low, preferred_element_type=F32) + bias_in[:, :, None]
    cdf = 0.5 * (1.0 + lax.erf(hidden * 0.5**0.5))
    active = (hidden * cdf).astype(BF)
    slope = cdf + hidden * jnp.exp(-0.5 * hidden * hidden) * 0.3989422804014327
    second_sum = (
        normed + jnp.einsum("cdf,cft->dt", full_out, active, preferred_element_type=F32) + bias_out[:, None]
    )
    result, xhat2, rstd2 = norm_forward(second_sum, gains[1], shifts[1])
    activations = lax.all_to_all((result * live).astype(BF), "col", split_axis=0, concat_axis=1, tiled=True)
    activations = activations.astype(F32)

    upstream = up.astype(F32) * live
    gain_two = jnp.sum(upstream * xhat2, axis=1)
    shift_two = jnp.sum(upstream, axis=1)
    d_second = norm_backward(upstream, xhat2, rstd2, gains[1])
    g_bias_out = jnp.sum(d_second, axis=1)
    d_second_low = d_second.astype(BF)
    g_out = jnp.einsum("dt,cft->cdf", d_second_low, active, preferred_element_type=F32)
    d_hidden = jnp.einsum("cdf,dt->cft", full_out, d_second_low, preferred_element_type=F32) * slope
    g_bias_in = jnp.sum(d_hidden, axis=2)
    d_hidden_low = d_hidden.astype(BF)
    g_in = jnp.einsum("dt,cft->cdf", normed_low, d_hidden_low, preferred_element_type=F32)
    g_both = jnp.stack([g_in.astype(BF).reshape(-1, rows, hid), g_out.astype(BF).reshape(-1, rows, hid)], axis=1)
    g_both = lax.psum_scatter(g_both, OWNERS, scatter_dimension=0, tiled=True).astype(F32)
    g_in, g_out = g_both[0, 0], g_both[0, 1]
    d_normed = d_second + jnp.einsum("cdf,cft->dt", full_in, d_hidden_low, preferred_element_type=F32)
    gain_one = jnp.sum(d_normed * xhat1, axis=1)
    shift_one = jnp.sum(d_normed, axis=1)
    d_first = norm_backward(d_normed, xhat1, rstd1, gains[0])
    g_bias_attn = jnp.sum(d_first, axis=1)
    d_first_low = d_first.astype(BF)
    d_attended = jnp.einsum("cde,dt->cet", full_attn, d_first_low, preferred_element_type=F32).astype(BF)
    d_attended = d_attended.reshape(heads, HEAD_DIM, SEQ_MAX)
    g_attn = jnp.einsum("dt,cet->cde", d_first_low, attended_cols, preferred_element_type=F32)
    d_qk, d_v, bias_sums = attend_backward(qk, values, key_mask, attended, total, d_attended)
    d_qk = d_qk.reshape(cols, 2 * width, SEQ_MAX)
    d_v = d_v.reshape(cols, width, SEQ_MAX)
    bias_sums = jnp.sum(bias_sums, axis=3)
    g_bias_q, g_bias_v = bias_sums[:, 0].reshape(d), bias_sums[:, 1].reshape(d)
    g_qk = jnp.einsum("dt,cnt->cdn", x, d_qk, preferred_element_type=F32)
    g_v = jnp.einsum("dt,cnt->cdn", x, d_v, preferred_element_type=F32)
    token_grad = (
        d_first + jnp.einsum("cdn,cnt->dt", full_qk, d_qk, preferred_element_type=F32)
        + jnp.einsum("cdn,cnt->dt", full_v, d_v, preferred_element_type=F32)
    )
    small = jnp.stack([g_bias_q, g_bias_v, g_bias_attn, g_bias_out, gain_one, gain_two, shift_one, shift_two])
    small = small.reshape(8, cols, width).transpose(1, 0, 2)
    small = jnp.concatenate([small, g_bias_in.reshape(cols, -1, width)], axis=1)
    near = dp_bits + row_bits[::-1] + col_bits
    far = dp_bits + row_bits + col_bits
    g_qk, g_v, g_attn, token_grad, own = tail(
        (near, far, far), [g.astype(BF) for g in (g_qk, g_v, g_attn)], token_grad.astype(BF), small
    )
    return (
        activations, token_grad, jnp.concatenate([g_qk, g_v], axis=1).reshape(rows, 3, width), own[0:2],
        g_attn, own[2], g_in, own[8:].reshape(hid), g_out, own[3], own[4:6], own[6:8],
    )


def solution(mesh):
    return jax.shard_map(
        local,
        mesh=mesh,
        in_specs=(
            P("col", ROWS), P(ROWS, None, "col"), P(None, "col"), P(ROWS, "col"), P("col"),
            P(ROWS, "col"), P("col"), P(ROWS, "col"), P("col"), P(None, "col"), P(None, "col"),
            P(ROWS), P(ROWS), P("col", ROWS),
        ),
        out_specs=(
            P("col", ROWS), P("col", ROWS), P(ROWS, None, "col"), P(None, "col"), P(ROWS, "col"),
            P("col"), P(ROWS, "col"), P("col"), P(ROWS, "col"), P("col"), P(None, "col"), P(None, "col"),
        ),
        check_vma=False,
    )
```

```python
import jax
import jax.numpy as jnp
from jax import lax
from jax.experimental import pallas as pl
from jax.experimental.pallas import tpu as pltpu
from jax.sharding import PartitionSpec as P

HEAD_DIM = 64
SEQ_MAX = 1024
EPSILON = 1e-12
ROWS = ("dp", "row")
ALL = ("dp", "row", "col")
OWNERS = ("col", "dp", "row")
BF = jnp.bfloat16
F32 = jnp.float32
LOG2E = 1.4426950408889634
SCALE = HEAD_DIM ** (-0.5)
QBLOCK = 256
EXTRA = 16


def dot_nn(a, b):
    return lax.dot_general(a, b, (((1,), (0,)), ((), ())), preferred_element_type=F32)


def dot_tn(a, b):
    return lax.dot_general(a, b, (((0,), (0,)), ((), ())), preferred_element_type=F32)


def dot_nt(a, b):
    return lax.dot_general(a, b, (((1,), (1,)), ((), ())), preferred_element_type=F32)


def mean_rows(v):
    return jnp.mean(v, axis=0, keepdims=True)


def norm_forward(values, gain, shift):
    centred = values - mean_rows(values)
    inverse = lax.rsqrt(mean_rows(centred * centred) + EPSILON)
    scaled = centred * inverse
    return scaled * gain[:, None] + shift[:, None], scaled, inverse


def norm_backward(upstream, scaled, inverse, gain):
    weighted = upstream * gain[:, None]
    return inverse * (weighted - mean_rows(weighted) - scaled * mean_rows(weighted * scaled))


def stack_rows(rows, width):
    place = lax.broadcasted_iota(jnp.int32, (EXTRA, width), 0)
    out = jnp.zeros((EXTRA, width), F32)
    for i, row in enumerate(rows):
        out = jnp.where(place == i, row, out)
    return out.astype(BF)


def three_parts(row):
    high = row.astype(BF).astype(F32)
    middle = (row - high).astype(BF).astype(F32)
    return high, middle, row - high - middle


def attend_backward_kernel(
    q_ref, k_ref, v_ref, mask_ref, out_ref, total_ref, up_ref,
    grad_qk_ref, grad_v_ref, bias_ref, dk_ref, dv_ref,
):
    seq = q_ref.shape[-1]
    one = jnp.ones((1, seq), F32)
    keys = k_ref[0, 0, 0]
    queries = q_ref[0, 0, 0]
    up = up_ref[0]
    delta = jnp.sum(up.astype(F32) * out_ref[0].astype(F32), axis=0, keepdims=True)
    key_side = jnp.concatenate([keys, stack_rows([mask_ref[...], one, one, one], seq)], axis=0).T
    value_side = jnp.concatenate([v_ref[0, 0, 0], stack_rows([one, one, one], seq)], axis=0).T
    query_side = jnp.concatenate([queries, stack_rows([one, *three_parts(-total_ref[0])], seq)], axis=0)
    up_side = jnp.concatenate([up, stack_rows(three_parts(-delta), seq)], axis=0)
    lanes = 128
    sum_q = jnp.zeros((HEAD_DIM, lanes), F32)
    for j in range(seq // QBLOCK):
        cols = slice(j * QBLOCK, (j + 1) * QBLOCK)
        weights = jnp.exp2(dot_nn(key_side, query_side[:, cols]) * (SCALE * LOG2E))
        d_scores = (weights * dot_nn(value_side, up_side[:, cols])).astype(BF)
        d_q = dot_nn(keys, d_scores) * SCALE
        for part in range(QBLOCK // lanes):
            sum_q += d_q[:, part * lanes : (part + 1) * lanes]
        grad_qk_ref[0, 0, 0, :, cols] = d_q.astype(BF)
        d_k = dot_nt(queries[:, cols], d_scores)
        d_v = dot_nt(up[:, cols], weights.astype(BF))
        if j == 0:
            dk_ref[...] = d_k
            dv_ref[...] = d_v
        else:
            dk_ref[...] += d_k
            dv_ref[...] += d_v
    grad_qk_ref[0, 1, 0] = (dk_ref[...] * SCALE).astype(BF)
    grad_v_ref[0, 0, 0] = dv_ref[...].astype(BF)
    bias_ref[0, 0] = sum_q
    sum_v = jnp.zeros((HEAD_DIM, lanes), F32)
    for part in range(seq // lanes):
        sum_v += dv_ref[:, part * lanes : (part + 1) * lanes]
    bias_ref[0, 1] = sum_v


def projection_spec(first, count, per_col, seq):
    return pl.BlockSpec((1, count, 1, HEAD_DIM, seq), lambda h: (h // per_col, first, h % per_col, 0, 0))


def head_spec(rows, seq):
    return pl.BlockSpec((1, rows, seq), lambda h: (h, 0, 0))


def qkv_specs(per_col, seq):
    return [
        projection_spec(0, 1, per_col, seq), projection_spec(1, 1, per_col, seq), projection_spec(0, 1, per_col, seq),
        pl.BlockSpec((1, seq), lambda h: (0, 0)),
    ]


def attend_backward(qk, v, mask, attended, total, d_attended):
    cols, _, per_col, _, seq = qk.shape
    heads = cols * per_col
    return pl.pallas_call(
        attend_backward_kernel,
        grid=(heads,),
        in_specs=qkv_specs(per_col, seq)
        + [head_spec(HEAD_DIM, seq), head_spec(1, seq), head_spec(HEAD_DIM, seq)],
        out_specs=[
            projection_spec(0, 2, per_col, seq),
            projection_spec(0, 1, per_col, seq),
            pl.BlockSpec((1, 2, HEAD_DIM, 128), lambda h: (h, 0, 0, 0)),
        ],
        out_shape=[
            jax.ShapeDtypeStruct(qk.shape, BF),
            jax.ShapeDtypeStruct(v.shape, BF),
            jax.ShapeDtypeStruct((heads, 2, HEAD_DIM, 128), F32),
        ],
        scratch_shapes=[pltpu.VMEM((HEAD_DIM, seq), F32), pltpu.VMEM((HEAD_DIM, seq), F32)],
        cost_estimate=pl.CostEstimate(
            flops=heads * seq * seq * HEAD_DIM * 40, bytes_accessed=heads * seq * HEAD_DIM * 16,
            transcendentals=heads * seq * seq,
        ),
        name="attend_backward",
    )(qk, qk, v, mask, attended, total, d_attended)


def axis_bits(name):
    size = lax.axis_size(name)
    return [(name, 1 << b) for b in reversed(range(size.bit_length() - 1))]


def my_bit(name, bit):
    return (lax.axis_index(name) // bit) % 2


def partner(name, bit):
    return {name: lax.axis_index(name) + bit * (1 - 2 * my_bit(name, bit))}


def all_bits():
    return axis_bits("col") + axis_bits("dp") + axis_bits("row")


def col_peer(step):
    cols = lax.axis_size("col")
    col = lax.axis_index("col")
    return (col + step) % cols, (col + cols - step) % cols


def remote(src, dst, send, recv, device):
    return pltpu.make_async_remote_copy(
        src_ref=src, dst_ref=dst, send_sem=send, recv_sem=recv, device_id=device,
        device_id_type=pl.DeviceIdType.MESH,
    )


def meet_partners():
    barrier = pltpu.get_barrier_semaphore()
    devices = [partner(name, bit) for name, bit in axis_bits("dp") + axis_bits("row")]
    devices += [{"col": col_peer(step)[0]} for step in range(1, lax.axis_size("col"))]
    for device in devices:
        pl.semaphore_signal(barrier, inc=1, device_id=device, device_id_type=pl.DeviceIdType.MESH)
    pl.semaphore_wait(barrier, len(devices))


def attend_forward_kernel(
    pieces, events, q_ref, k_ref, v_ref, mask_ref, *refs
):
    count = 1 + max(which for which, _, _ in pieces)
    shards, (out_ref, total_ref), fulls = refs[:count], refs[count : count + 2], refs[count + 2 : 2 * count + 2]
    own_sem, block_send, block_recv = refs[2 * count + 2 :]
    dims = all_bits()
    levels = len(dims)
    head = pl.program_id(0)
    place = [my_bit(name, bit) for name, bit in dims]

    def stage(piece, step):
        which, cols, order = pieces[piece]
        index = tuple(slice(None) if bit in order[:step] else at for bit, at in zip(dims, place))
        target = fulls[which].at[index + (slice(None), cols)]
        return remote(
            shards[which].at[:, cols] if step == 0 else target, target, block_send.at[piece, step],
            block_recv.at[piece, step], partner(*order[step]),
        )

    def own(which):
        return pltpu.make_async_copy(shards[which], fulls[which].at[tuple(place)], own_sem.at[which])

    def advance(piece, step):
        stage(piece, step).wait()
        if step + 1 < levels:
            stage(piece, step + 1).start()

    @pl.when(head == 0)
    def _():
        for which in range(count):
            own(which).start()
        meet_partners()
        for piece in range(len(pieces)):
            stage(piece, 0).start()
        for which in range(count):
            own(which).wait()

    for at, moves in events:
        if at >= 0:

            @pl.when(head == at)
            def _(moves=moves):
                for piece, step in moves:
                    advance(piece, step)

    seq = q_ref.shape[-1]
    one = jnp.ones((1, seq), F32)
    keys = jnp.concatenate([k_ref[0, 0, 0], stack_rows([mask_ref[...]], seq)], axis=0).T
    queries = jnp.concatenate([q_ref[0, 0, 0], stack_rows([one], seq)], axis=0)
    values = v_ref[0, 0, 0]
    for j in range(seq // QBLOCK):
        cols = slice(j * QBLOCK, (j + 1) * QBLOCK)
        scores = dot_nn(keys, queries[:, cols])
        largest = jnp.max(scores, axis=0, keepdims=True)
        exponent = jnp.exp2((scores - largest) * (SCALE * LOG2E))
        total = jnp.sum(exponent, axis=0, keepdims=True)
        weights = (exponent * (1.0 / total)).astype(BF)
        out_ref[0, :, cols] = dot_nn(values, weights).astype(BF)
        total_ref[0, :, cols] = largest + jnp.log(total) * (1.0 / SCALE)

    @pl.when(head == pl.num_programs(0) - 1)
    def _():
        for at, moves in events:
            if at < 0:
                for piece, step in moves:
                    advance(piece, step)


def head_kernel(
    orders, qk_ref, vo_ref, tokens_ref, vectors_ref, full_qk_ref, full_vo_ref, x_ref, all_vectors_ref,
    own_sem, block_send, block_recv, col_send, col_recv,
):
    dims = all_bits()
    cols, col = lax.axis_size("col"), lax.axis_index("col")
    feats, seq = tokens_ref.shape[0], x_ref.shape[1]
    place = [my_bit(name, bit) for name, bit in dims]
    pieces = [(qk_ref, full_qk_ref), (vo_ref, full_vo_ref)]
    my_feats = pl.ds(pl.multiple_of(col * feats, 8), feats)
    own = [pltpu.make_async_copy(src, dst.at[tuple(place)], own_sem.at[i]) for i, (src, dst) in enumerate(pieces)]
    own.append(
        pltpu.make_async_copy(
            tokens_ref.at[:, pl.ds(pl.multiple_of(col * seq, 128), seq)], x_ref.at[my_feats], own_sem.at[2]
        )
    )
    own.append(pltpu.make_async_copy(vectors_ref, all_vectors_ref.at[col], own_sem.at[3]))
    for copy in own:
        copy.start()
    meet_partners()

    def stage(piece, step):
        src, full = pieces[piece]
        done = orders[piece][:step]
        index = tuple(slice(None) if bit in done else at for bit, at in zip(dims, place))
        return remote(
            src if step == 0 else full.at[index], full.at[index], block_send.at[piece, step],
            block_recv.at[piece, step], partner(*orders[piece][step]),
        )

    stages = [[stage(piece, step) for step in range(len(dims))] for piece in range(2)]
    for piece in range(2):
        stages[piece][0].start()
    transposes = []
    for step in range(1, cols):
        to, _ = col_peer(step)
        transposes.append(
            remote(vectors_ref, all_vectors_ref.at[col], col_send.at[0, step], col_recv.at[0, step], {"col": to})
        )
        transposes.append(
            remote(
                tokens_ref.at[:, pl.ds(pl.multiple_of(to * seq, 128), seq)], x_ref.at[my_feats],
                col_send.at[1, step], col_recv.at[1, step], {"col": to},
            )
        )
    for copy in transposes:
        copy.start()
    for copy in own:
        copy.wait()
    for step in range(len(dims)):
        for piece in range(2):
            stages[piece][step].wait()
            if step + 1 < len(dims):
                stages[piece][step + 1].start()
    for copy in transposes:
        copy.wait()


def head(orders, qk, vo, tokens, vectors):
    dims = all_bits()
    cols = lax.axis_size("col")
    twos = (2,) * len(dims)
    vmem = pl.BlockSpec(memory_space=pltpu.VMEM)
    return pl.pallas_call(
        lambda *refs: head_kernel(orders, *refs),
        in_specs=[vmem] * 4,
        out_specs=[vmem] * 4,
        out_shape=[
            jax.ShapeDtypeStruct(twos + qk.shape, BF),
            jax.ShapeDtypeStruct(twos + vo.shape, BF),
            jax.ShapeDtypeStruct((cols * tokens.shape[0], SEQ_MAX), BF),
            jax.ShapeDtypeStruct((cols,) + vectors.shape, F32),
        ],
        scratch_shapes=[
            pltpu.SemaphoreType.DMA((4,)),
            pltpu.SemaphoreType.DMA((2, len(dims))), pltpu.SemaphoreType.DMA((2, len(dims))),
            pltpu.SemaphoreType.DMA((2, cols)), pltpu.SemaphoreType.DMA((2, cols)),
        ],
        compiler_params=pltpu.CompilerParams(collective_id=0, has_side_effects=True),
        name="head",
    )(qk, vo, tokens, vectors)


def attend_forward(qk, v, mask, shards, orders):
    cols, _, per_col, _, seq = qk.shape
    heads = cols * per_col
    dims = all_bits()
    levels = len(dims)
    half = shards[0].shape[1] // len(orders)
    pieces = [
        (which, pl.ds(k * half, half), orders[k]) for which in range(len(shards)) for k in range(len(orders))
    ]
    first, second = [0, 1], [2, 3]
    events = [(1, [(p, 0) for p in first]), (5, [(p, 1) for p in first] + [(p, 0) for p in second])]
    events += [(7, [(p, 2) for p in first]), (9, [(p, 1) for p in second])]
    for step in range(3, levels + 1):
        events.append((-1, [(p, step) for p in first if step < levels] + [(p, step - 1) for p in second]))
    twos = (2,) * levels
    return pl.pallas_call(
        lambda *refs: attend_forward_kernel(pieces, events, *refs),
        grid=(heads,),
        in_specs=qkv_specs(per_col, seq) + [pl.BlockSpec(a.shape, lambda h: (0, 0)) for a in shards],
        out_specs=[head_spec(HEAD_DIM, seq), head_spec(1, seq)] + [pl.BlockSpec(memory_space=pl.ANY)] * len(shards),
        out_shape=[
            jax.ShapeDtypeStruct((heads, HEAD_DIM, seq), BF),
            jax.ShapeDtypeStruct((heads, 1, seq), F32),
        ]
        + [jax.ShapeDtypeStruct(twos + a.shape, BF) for a in shards],
        scratch_shapes=[
            pltpu.SemaphoreType.DMA((len(shards),)),
            pltpu.SemaphoreType.DMA((len(pieces), levels)), pltpu.SemaphoreType.DMA((len(pieces), levels)),
        ],
        compiler_params=pltpu.CompilerParams(collective_id=2, has_side_effects=True),
        cost_estimate=pl.CostEstimate(
            flops=heads * seq * seq * HEAD_DIM * 16, bytes_accessed=heads * seq * HEAD_DIM * 8,
            transcendentals=heads * seq * seq,
        ),
        name="attend_forward",
    )(qk, qk, v, mask, *shards)


def tail_kernel(orders, *refs):
    dims = all_bits()
    levels = len(dims)
    count = len(orders)
    cols, col = lax.axis_size("col"), lax.axis_index("col")
    grads, (token_ref, small_ref) = refs[:count], refs[count : count + 2]
    refs = refs[count + 2 :]
    sums, (out_ref, own_ref) = refs[:count], refs[count : count + 2]
    refs = refs[count + 2 :]
    landed = [refs[i * levels : (i + 1) * levels] for i in range(count)]
    refs = refs[count * levels :]
    (
        token_landed, small_landed, small_sum, block_send, block_recv, col_send, col_recv, small_send, small_recv,
    ) = refs
    feats, seq = token_landed.shape[1], token_landed.shape[2]
    small_bits = axis_bits("row") + axis_bits("dp")
    meet_partners()

    def views(piece, step):
        left = [bit for bit in dims if bit not in orders[piece][:step]]
        axis = left.index(orders[piece][step])
        return grads[piece] if step == 0 else landed[piece][step - 1], axis, my_bit(*orders[piece][step])

    def stage(piece, step):
        operand, axis, mine = views(piece, step)
        return remote(
            operand.at[(slice(None),) * axis + (1 - mine,)], landed[piece][step], block_send.at[piece, step],
            block_recv.at[piece, step], partner(*orders[piece][step]),
        )

    def add(piece, step):
        operand, axis, mine = views(piece, step)
        arrived = landed[piece][step]
        free = levels - 1 - step

        def body(i, carry):
            index = [(i // 2 ** (free - 1 - k)) % 2 for k in range(free)]
            kept = operand[tuple(index[:axis] + [mine] + index[axis:])].astype(F32)
            total = kept + arrived[tuple(index)].astype(F32)
            if free:
                arrived[tuple(index)] = total.astype(BF)
            else:
                sums[piece][...] = total
            return carry

        if free:
            lax.fori_loop(0, 2**free, body, 0)
        else:
            body(0, 0)

    stages = [[stage(piece, step) for step in range(levels)] for piece in range(count)]
    for piece in range(count):
        stages[piece][0].start()
    small_copies = []
    token_copies = []
    for step in range(1, cols):
        to, _ = col_peer(step)
        small_copies.append(
            remote(small_ref.at[to], small_landed.at[step], col_send.at[0, step], col_recv.at[0, step], {"col": to})
        )
        token_copies.append(
            remote(
                token_ref.at[pl.ds(pl.multiple_of(to * feats, 8), feats)], token_landed.at[step],
                col_send.at[1, step], col_recv.at[1, step], {"col": to},
            )
        )
    for copy in small_copies + token_copies:
        copy.start()
    out_ref[:, pl.ds(pl.multiple_of(col * seq, 128), seq)] = token_ref[
        pl.ds(pl.multiple_of(col * feats, 8), feats)
    ].astype(F32)
    for copy in small_copies:
        copy.wait()
    total = small_ref[col]
    for step in range(1, cols):
        total = total + small_landed[step]
    small_sum[0] = total
    for step in range(max(levels, len(small_bits))):
        if step < len(small_bits):
            small_copy = remote(
                small_sum.at[step], small_landed.at[cols + step], small_send.at[step], small_recv.at[step],
                partner(*small_bits[step]),
            )
            small_copy.start()
        for piece in range(count):
            if step < levels:
                stages[piece][step].wait()
                add(piece, step)
                if step + 1 < levels:
                    stages[piece][step + 1].start()
        if step < len(small_bits):
            small_copy.wait()
            small_sum[step + 1] = small_sum[step] + small_landed[cols + step]
    own_ref[...] = small_sum[len(small_bits)]
    for step in range(1, cols):
        _, source = col_peer(step)
        token_copies[step - 1].wait()
        out_ref[:, pl.ds(pl.multiple_of(source * seq, 128), seq)] = token_landed[step].astype(F32)


def tail(orders, grads, token_grad, small):
    dims = all_bits()
    levels = len(dims)
    cols = lax.axis_size("col")
    rows = grads[0].shape[0] * grads[0].shape[1] >> levels
    feats = token_grad.shape[0] // cols
    grads = [g.reshape((2,) * levels + (rows, g.shape[2])) for g in grads]
    widths = [g.shape[-1] for g in grads]
    small_bits = axis_bits("row") + axis_bits("dp")
    vmem = pl.BlockSpec(memory_space=pltpu.VMEM)
    dma = pltpu.SemaphoreType.DMA
    return pl.pallas_call(
        lambda *refs: tail_kernel(orders, *refs),
        in_specs=[vmem] * (len(grads) + 2),
        out_specs=[vmem] * (len(grads) + 2),
        out_shape=[jax.ShapeDtypeStruct((rows, w), F32) for w in widths]
        + [jax.ShapeDtypeStruct((feats, cols * SEQ_MAX), F32), jax.ShapeDtypeStruct(small.shape[1:], F32)],
        scratch_shapes=[
            pltpu.VMEM((2,) * (levels - 1 - step) + (rows, w), BF) for w in widths for step in range(levels)
        ]
        + [
            pltpu.VMEM((cols, feats, SEQ_MAX), BF),
            pltpu.VMEM((cols + len(small_bits),) + small.shape[1:], F32),
            pltpu.VMEM((len(small_bits) + 1,) + small.shape[1:], F32),
            dma((len(grads), levels)), dma((len(grads), levels)), dma((2, cols)), dma((2, cols)),
            dma((len(small_bits),)), dma((len(small_bits),)),
        ],
        compiler_params=pltpu.CompilerParams(collective_id=1, has_side_effects=True),
        name="tail",
    )(*grads, token_grad, small)


def local(
    tokens, w_qkv, bias_qv, w_attn_out, bias_attn_out, w_in, bias_in, w_out, bias_out,
    norm_gains, norm_biases, seq_lengths, seq_offsets, cotangent,
):
    cols = lax.axis_size("col")
    col = lax.axis_index("col")
    rows, _, width = w_qkv.shape
    groups = lax.axis_size("dp") * lax.axis_size("row")
    d = rows * groups
    heads = d // HEAD_DIM
    hid = w_in.shape[1]

    col_bits, row_bits, dp_bits = axis_bits("col"), axis_bits("row"), axis_bits("dp")
    near_first = col_bits[::-1] + row_bits[::-1] + dp_bits
    far_first = col_bits[::-1] + row_bits + dp_bits

    vectors = jnp.concatenate(
        [bias_qv, bias_attn_out[None], bias_out[None], norm_gains, norm_biases, bias_in.reshape(-1, width)], axis=0
    )
    w_flat = w_qkv.reshape(rows, 3 * width)
    w_vo = jnp.concatenate([w_flat[:, 2 * width :], w_attn_out], axis=1)
    full_qk, full_vo, x, vectors = head((near_first, far_first), w_flat[:, : 2 * width], w_vo, tokens, vectors)
    full_qk = full_qk.reshape(cols, d, 2 * width)
    full_vo = full_vo.reshape(cols, d, 2 * width)
    full_v = full_vo[:, :, :width]
    full_attn = full_vo[:, :, width:]
    bias_q, bias_v = vectors[:, 0], vectors[:, 1]
    bias_attn_out, bias_out = vectors[:, 2].reshape(d), vectors[:, 3].reshape(d)
    gains = [vectors[:, 4].reshape(d), vectors[:, 5].reshape(d)]
    shifts = [vectors[:, 6].reshape(d), vectors[:, 7].reshape(d)]
    bias_in = vectors[:, 8:].reshape(cols, hid)

    def to_window(a):
        return lax.all_to_all(a, "col", split_axis=1, concat_axis=0, tiled=True)

    length = lax.dynamic_index_in_dim(seq_lengths, col, keepdims=False)
    offset = lax.dynamic_index_in_dim(seq_offsets, col, keepdims=False)
    places = lax.broadcasted_iota(jnp.int32, (1, SEQ_MAX), 1)
    live_mask = (places >= offset) & (places < offset + length)
    live = live_mask.astype(F32)
    key_mask = jnp.where(live_mask, 0.0, -1e30).astype(F32)

    def project(weights, shift):
        out = jnp.einsum("cdn,dt->cnt", weights, x, preferred_element_type=F32) + shift[:, :, None]
        return out.astype(BF).reshape(cols, -1, width // HEAD_DIM, HEAD_DIM, SEQ_MAX)

    qk = project(full_qk, jnp.concatenate([bias_q, jnp.zeros_like(bias_q)], axis=1))
    values = project(full_v, bias_v)
    attended, total, full_in, full_out = attend_forward(
        qk, values, key_mask, (w_in, w_out), (near_first, far_first)
    )
    full_in = full_in.reshape(cols, d, hid)
    full_out = full_out.reshape(cols, d, hid)
    attended, cotangent = lax.optimization_barrier((attended, cotangent))
    up = to_window(cotangent)
    attended_cols = attended.reshape(cols, width, SEQ_MAX)
    first_sum = (
        x.astype(F32) + jnp.einsum("cde,cet->dt", full_attn, attended_cols, preferred_element_type=F32)
        + bias_attn_out[:, None]
    )
    normed, xhat1, rstd1 = norm_forward(first_sum, gains[0], shifts[0])
    normed_low = normed.astype(BF)
    hidden = jnp.einsum("cdf,dt->cft", full_in, normed_low, preferred_element_type=F32) + bias_in[:, :, None]
    cdf = 0.5 * (1.0 + lax.erf(hidden * 0.5**0.5))
    active = (hidden * cdf).astype(BF)
    slope = cdf + hidden * jnp.exp(-0.5 * hidden * hidden) * 0.3989422804014327
    second_sum = (
        normed + jnp.einsum("cdf,cft->dt", full_out, active, preferred_element_type=F32) + bias_out[:, None]
    )
    result, xhat2, rstd2 = norm_forward(second_sum, gains[1], shifts[1])
    activations = lax.all_to_all((result * live).astype(BF), "col", split_axis=0, concat_axis=1, tiled=True)
    activations = activations.astype(F32)

    upstream = up.astype(F32) * live
    gain_two = jnp.sum(upstream * xhat2, axis=1)
    shift_two = jnp.sum(upstream, axis=1)
    d_second = norm_backward(upstream, xhat2, rstd2, gains[1])
    g_bias_out = jnp.sum(d_second, axis=1)
    d_second_low = d_second.astype(BF)
    g_out = jnp.einsum("dt,cft->cdf", d_second_low, active, preferred_element_type=F32)
    d_hidden = jnp.einsum("cdf,dt->cft", full_out, d_second_low, preferred_element_type=F32) * slope
    g_bias_in = jnp.sum(d_hidden, axis=2)
    d_hidden_low = d_hidden.astype(BF)
    g_in = jnp.einsum("dt,cft->cdf", normed_low, d_hidden_low, preferred_element_type=F32)
    g_both = jnp.stack([g_in.astype(BF).reshape(-1, rows, hid), g_out.astype(BF).reshape(-1, rows, hid)], axis=1)
    g_both = lax.psum_scatter(g_both, OWNERS, scatter_dimension=0, tiled=True).astype(F32)
    g_in, g_out = g_both[0, 0], g_both[0, 1]
    d_normed = d_second + jnp.einsum("cdf,cft->dt", full_in, d_hidden_low, preferred_element_type=F32)
    gain_one = jnp.sum(d_normed * xhat1, axis=1)
    shift_one = jnp.sum(d_normed, axis=1)
    d_first = norm_backward(d_normed, xhat1, rstd1, gains[0])
    g_bias_attn = jnp.sum(d_first, axis=1)
    d_first_low = d_first.astype(BF)
    d_attended = jnp.einsum("cde,dt->cet", full_attn, d_first_low, preferred_element_type=F32).astype(BF)
    d_attended = d_attended.reshape(heads, HEAD_DIM, SEQ_MAX)
    g_attn = jnp.einsum("dt,cet->cde", d_first_low, attended_cols, preferred_element_type=F32)
    d_qk, d_v, bias_sums = attend_backward(qk, values, key_mask, attended, total, d_attended)
    d_qk = d_qk.reshape(cols, 2 * width, SEQ_MAX)
    d_v = d_v.reshape(cols, width, SEQ_MAX)
    bias_sums = jnp.sum(bias_sums, axis=3)
    g_bias_q, g_bias_v = bias_sums[:, 0].reshape(d), bias_sums[:, 1].reshape(d)
    g_qk = jnp.einsum("dt,cnt->cdn", x, d_qk, preferred_element_type=F32)
    g_v = jnp.einsum("dt,cnt->cdn", x, d_v, preferred_element_type=F32)
    token_grad = (
        d_first + jnp.einsum("cdn,cnt->dt", full_qk, d_qk, preferred_element_type=F32)
        + jnp.einsum("cdn,cnt->dt", full_v, d_v, preferred_element_type=F32)
    )
    small = jnp.stack([g_bias_q, g_bias_v, g_bias_attn, g_bias_out, gain_one, gain_two, shift_one, shift_two])
    small = small.reshape(8, cols, width).transpose(1, 0, 2)
    small = jnp.concatenate([small, g_bias_in.reshape(cols, -1, width)], axis=1)
    near = dp_bits + row_bits[::-1] + col_bits
    far = dp_bits + row_bits + col_bits
    g_qk, g_v, g_attn, token_grad, own = tail(
        (near, far, far), [g.astype(BF) for g in (g_qk, g_v, g_attn)], token_grad.astype(BF), small
    )
    return (
        activations, token_grad, jnp.concatenate([g_qk, g_v], axis=1).reshape(rows, 3, width), own[0:2],
        g_attn, own[2], g_in, own[8:].reshape(hid), g_out, own[3], own[4:6], own[6:8],
    )


def solution(mesh):
    return jax.shard_map(
        local,
        mesh=mesh,
        in_specs=(
            P("col", ROWS), P(ROWS, None, "col"), P(None, "col"), P(ROWS, "col"), P("col"),
            P(ROWS, "col"), P("col"), P(ROWS, "col"), P("col"), P(None, "col"), P(None, "col"),
            P(ROWS), P(ROWS), P("col", ROWS),
        ),
        out_specs=(
            P("col", ROWS), P("col", ROWS), P(ROWS, None, "col"), P(None, "col"), P(ROWS, "col"),
            P("col"), P(ROWS, "col"), P("col"), P(ROWS, "col"), P("col"), P(None, "col"), P(None, "col"),
        ),
        check_vma=False,
    )
```

```python
import jax
import jax.numpy as jnp
from jax import lax
from jax.experimental import pallas as pl
from jax.experimental.pallas import tpu as pltpu
from jax.sharding import PartitionSpec as P

HEAD_DIM = 64
SEQ_MAX = 1024
EPSILON = 1e-12
ROWS = ("dp", "row")
ALL = ("dp", "row", "col")
OWNERS = ("col", "dp", "row")
BF = jnp.bfloat16
F32 = jnp.float32
LOG2E = 1.4426950408889634
SCALE = HEAD_DIM ** (-0.5)
QBLOCK = 256
EXTRA = 16


def dot_nn(a, b):
    return lax.dot_general(a, b, (((1,), (0,)), ((), ())), preferred_element_type=F32)


def dot_tn(a, b):
    return lax.dot_general(a, b, (((0,), (0,)), ((), ())), preferred_element_type=F32)


def dot_nt(a, b):
    return lax.dot_general(a, b, (((1,), (1,)), ((), ())), preferred_element_type=F32)


def mean_rows(v):
    return jnp.mean(v, axis=0, keepdims=True)


def norm_forward(values, gain, shift):
    centred = values - mean_rows(values)
    inverse = lax.rsqrt(mean_rows(centred * centred) + EPSILON)
    scaled = centred * inverse
    return scaled * gain[:, None] + shift[:, None], scaled, inverse


def norm_backward(upstream, scaled, inverse, gain):
    weighted = upstream * gain[:, None]
    return inverse * (weighted - mean_rows(weighted) - scaled * mean_rows(weighted * scaled))


def stack_rows(rows, width):
    place = lax.broadcasted_iota(jnp.int32, (EXTRA, width), 0)
    out = jnp.zeros((EXTRA, width), F32)
    for i, row in enumerate(rows):
        out = jnp.where(place == i, row, out)
    return out.astype(BF)


def three_parts(row):
    high = row.astype(BF).astype(F32)
    middle = (row - high).astype(BF).astype(F32)
    return high, middle, row - high - middle


def attend_backward_kernel(
    q_ref, k_ref, v_ref, mask_ref, out_ref, total_ref, up_ref,
    grad_qk_ref, grad_v_ref, bias_ref, dk_ref, dv_ref,
):
    seq = q_ref.shape[-1]
    one = jnp.ones((1, seq), F32)
    keys = k_ref[0, 0, 0]
    queries = q_ref[0, 0, 0]
    up = up_ref[0]
    delta = jnp.sum(up.astype(F32) * out_ref[0].astype(F32), axis=0, keepdims=True)
    key_side = jnp.concatenate([keys, stack_rows([mask_ref[...], one, one, one], seq)], axis=0).T
    value_side = jnp.concatenate([v_ref[0, 0, 0], stack_rows([one, one, one], seq)], axis=0).T
    query_side = jnp.concatenate([queries, stack_rows([one, *three_parts(-total_ref[0])], seq)], axis=0)
    up_side = jnp.concatenate([up, stack_rows(three_parts(-delta), seq)], axis=0)
    lanes = 128
    sum_q = jnp.zeros((HEAD_DIM, lanes), F32)
    for j in range(seq // QBLOCK):
        cols = slice(j * QBLOCK, (j + 1) * QBLOCK)
        weights = jnp.exp2(dot_nn(key_side, query_side[:, cols]) * (SCALE * LOG2E))
        d_scores = (weights * dot_nn(value_side, up_side[:, cols])).astype(BF)
        d_q = dot_nn(keys, d_scores) * SCALE
        for part in range(QBLOCK // lanes):
            sum_q += d_q[:, part * lanes : (part + 1) * lanes]
        grad_qk_ref[0, 0, 0, :, cols] = d_q.astype(BF)
        d_k = dot_nt(queries[:, cols], d_scores)
        d_v = dot_nt(up[:, cols], weights.astype(BF))
        if j == 0:
            dk_ref[...] = d_k
            dv_ref[...] = d_v
        else:
            dk_ref[...] += d_k
            dv_ref[...] += d_v
    grad_qk_ref[0, 1, 0] = (dk_ref[...] * SCALE).astype(BF)
    grad_v_ref[0, 0, 0] = dv_ref[...].astype(BF)
    bias_ref[0, 0] = sum_q
    sum_v = jnp.zeros((HEAD_DIM, lanes), F32)
    for part in range(seq // lanes):
        sum_v += dv_ref[:, part * lanes : (part + 1) * lanes]
    bias_ref[0, 1] = sum_v


def projection_spec(first, count, per_col, seq):
    return pl.BlockSpec((1, count, 1, HEAD_DIM, seq), lambda h: (h // per_col, first, h % per_col, 0, 0))


def head_spec(rows, seq):
    return pl.BlockSpec((1, rows, seq), lambda h: (h, 0, 0))


def qkv_specs(per_col, seq):
    return [
        projection_spec(0, 1, per_col, seq), projection_spec(1, 1, per_col, seq), projection_spec(0, 1, per_col, seq),
        pl.BlockSpec((1, seq), lambda h: (0, 0)),
    ]


def attend_backward(qk, v, mask, attended, total, d_attended):
    cols, _, per_col, _, seq = qk.shape
    heads = cols * per_col
    return pl.pallas_call(
        attend_backward_kernel,
        grid=(heads,),
        in_specs=qkv_specs(per_col, seq)
        + [head_spec(HEAD_DIM, seq), head_spec(1, seq), head_spec(HEAD_DIM, seq)],
        out_specs=[
            projection_spec(0, 2, per_col, seq),
            projection_spec(0, 1, per_col, seq),
            pl.BlockSpec((1, 2, HEAD_DIM, 128), lambda h: (h, 0, 0, 0)),
        ],
        out_shape=[
            jax.ShapeDtypeStruct(qk.shape, BF),
            jax.ShapeDtypeStruct(v.shape, BF),
            jax.ShapeDtypeStruct((heads, 2, HEAD_DIM, 128), F32),
        ],
        scratch_shapes=[pltpu.VMEM((HEAD_DIM, seq), F32), pltpu.VMEM((HEAD_DIM, seq), F32)],
        cost_estimate=pl.CostEstimate(
            flops=heads * seq * seq * HEAD_DIM * 40, bytes_accessed=heads * seq * HEAD_DIM * 16,
            transcendentals=heads * seq * seq,
        ),
        name="attend_backward",
    )(qk, qk, v, mask, attended, total, d_attended)


def axis_bits(name):
    size = lax.axis_size(name)
    return [(name, 1 << b) for b in reversed(range(size.bit_length() - 1))]


def my_bit(name, bit):
    return (lax.axis_index(name) // bit) % 2


def partner(name, bit):
    return {name: lax.axis_index(name) + bit * (1 - 2 * my_bit(name, bit))}


def all_bits():
    return axis_bits("col") + axis_bits("dp") + axis_bits("row")


def col_peer(step):
    cols = lax.axis_size("col")
    col = lax.axis_index("col")
    return (col + step) % cols, (col + cols - step) % cols


def remote(src, dst, send, recv, device):
    return pltpu.make_async_remote_copy(
        src_ref=src, dst_ref=dst, send_sem=send, recv_sem=recv, device_id=device,
        device_id_type=pl.DeviceIdType.MESH,
    )


def meet_partners():
    barrier = pltpu.get_barrier_semaphore()
    devices = [partner(name, bit) for name, bit in axis_bits("dp") + axis_bits("row")]
    devices += [{"col": col_peer(step)[0]} for step in range(1, lax.axis_size("col"))]
    for device in devices:
        pl.semaphore_signal(barrier, inc=1, device_id=device, device_id_type=pl.DeviceIdType.MESH)
    pl.semaphore_wait(barrier, len(devices))


def attend_forward_kernel(
    pieces, events, q_ref, k_ref, v_ref, mask_ref, *refs
):
    count = 1 + max(which for which, _, _ in pieces)
    shards, cotangent_ref, refs = refs[:count], refs[count], refs[count + 1 :]
    (out_ref, total_ref), fulls, up_ref = refs[:2], refs[2 : count + 2], refs[count + 2]
    own_sem, block_send, block_recv, col_send, col_recv = refs[count + 3 :]
    group, col = lax.axis_size("col"), lax.axis_index("col")
    feats, window = cotangent_ref.shape[0], up_ref.shape[1]
    dims = all_bits()
    levels = len(dims)
    head = pl.program_id(0)
    place = [my_bit(name, bit) for name, bit in dims]

    def stage(piece, step):
        which, cols, order = pieces[piece]
        index = tuple(slice(None) if bit in order[:step] else at for bit, at in zip(dims, place))
        target = fulls[which].at[index + (slice(None), cols)]
        return remote(
            shards[which].at[:, cols] if step == 0 else target, target, block_send.at[piece, step],
            block_recv.at[piece, step], partner(*order[step]),
        )

    def own(which):
        return pltpu.make_async_copy(shards[which], fulls[which].at[tuple(place)], own_sem.at[which])

    def transpose(step):
        to, _ = col_peer(step)
        src = cotangent_ref.at[:, pl.ds(pl.multiple_of(to * window, 128), window)]
        dst = up_ref.at[pl.ds(pl.multiple_of(col * feats, 8), feats)]
        if step == 0:
            return pltpu.make_async_copy(src, dst, own_sem.at[count])
        return remote(src, dst, col_send.at[step], col_recv.at[step], {"col": to})

    def advance(piece, step):
        if piece < 0:
            for k in range(1, group):
                transpose(k).start() if step == 0 else transpose(k).wait()
            return
        stage(piece, step).wait()
        if step + 1 < levels:
            stage(piece, step + 1).start()

    @pl.when(head == 0)
    def _():
        for which in range(count):
            own(which).start()
        transpose(0).start()
        meet_partners()
        for piece in range(len(pieces)):
            stage(piece, 0).start()
        for which in range(count):
            own(which).wait()
        transpose(0).wait()

    for at, moves in events:
        if at >= 0:

            @pl.when(head == at)
            def _(moves=moves):
                for piece, step in moves:
                    advance(piece, step)

    seq = q_ref.shape[-1]
    one = jnp.ones((1, seq), F32)
    keys = jnp.concatenate([k_ref[0, 0, 0], stack_rows([mask_ref[...]], seq)], axis=0).T
    queries = jnp.concatenate([q_ref[0, 0, 0], stack_rows([one], seq)], axis=0)
    values = v_ref[0, 0, 0]
    for j in range(seq // QBLOCK):
        cols = slice(j * QBLOCK, (j + 1) * QBLOCK)
        scores = dot_nn(keys, queries[:, cols])
        largest = jnp.max(scores, axis=0, keepdims=True)
        exponent = jnp.exp2((scores - largest) * (SCALE * LOG2E))
        total = jnp.sum(exponent, axis=0, keepdims=True)
        weights = (exponent * (1.0 / total)).astype(BF)
        out_ref[0, :, cols] = dot_nn(values, weights).astype(BF)
        total_ref[0, :, cols] = largest + jnp.log(total) * (1.0 / SCALE)

    @pl.when(head == pl.num_programs(0) - 1)
    def _():
        for at, moves in events:
            if at < 0:
                for piece, step in moves:
                    advance(piece, step)


def head_kernel(
    orders, qk_ref, vo_ref, tokens_ref, vectors_ref, full_qk_ref, full_vo_ref, x_ref, all_vectors_ref,
    own_sem, block_send, block_recv, col_send, col_recv,
):
    dims = all_bits()
    cols, col = lax.axis_size("col"), lax.axis_index("col")
    feats, seq = tokens_ref.shape[0], x_ref.shape[1]
    place = [my_bit(name, bit) for name, bit in dims]
    pieces = [(qk_ref, full_qk_ref), (vo_ref, full_vo_ref)]
    my_feats = pl.ds(pl.multiple_of(col * feats, 8), feats)
    own = [pltpu.make_async_copy(src, dst.at[tuple(place)], own_sem.at[i]) for i, (src, dst) in enumerate(pieces)]
    own.append(
        pltpu.make_async_copy(
            tokens_ref.at[:, pl.ds(pl.multiple_of(col * seq, 128), seq)], x_ref.at[my_feats], own_sem.at[2]
        )
    )
    own.append(pltpu.make_async_copy(vectors_ref, all_vectors_ref.at[col], own_sem.at[3]))
    for copy in own:
        copy.start()
    meet_partners()

    def stage(piece, step):
        src, full = pieces[piece]
        done = orders[piece][:step]
        index = tuple(slice(None) if bit in done else at for bit, at in zip(dims, place))
        return remote(
            src if step == 0 else full.at[index], full.at[index], block_send.at[piece, step],
            block_recv.at[piece, step], partner(*orders[piece][step]),
        )

    stages = [[stage(piece, step) for step in range(len(dims))] for piece in range(2)]
    for piece in range(2):
        stages[piece][0].start()
    transposes = []
    for step in range(1, cols):
        to, _ = col_peer(step)
        transposes.append(
            remote(vectors_ref, all_vectors_ref.at[col], col_send.at[0, step], col_recv.at[0, step], {"col": to})
        )
        transposes.append(
            remote(
                tokens_ref.at[:, pl.ds(pl.multiple_of(to * seq, 128), seq)], x_ref.at[my_feats],
                col_send.at[1, step], col_recv.at[1, step], {"col": to},
            )
        )
    for copy in transposes[::2]:
        copy.start()
    for copy in own:
        copy.wait()
    for step in range(len(dims)):
        for piece in range(2):
            stages[piece][step].wait()
            if step + 1 < len(dims):
                stages[piece][step + 1].start()
        if step + 1 == len(axis_bits("col")):
            for copy in transposes[1::2]:
                copy.start()
    for copy in transposes:
        copy.wait()


def head(orders, qk, vo, tokens, vectors):
    dims = all_bits()
    cols = lax.axis_size("col")
    twos = (2,) * len(dims)
    vmem = pl.BlockSpec(memory_space=pltpu.VMEM)
    return pl.pallas_call(
        lambda *refs: head_kernel(orders, *refs),
        in_specs=[vmem] * 4,
        out_specs=[vmem] * 4,
        out_shape=[
            jax.ShapeDtypeStruct(twos + qk.shape, BF),
            jax.ShapeDtypeStruct(twos + vo.shape, BF),
            jax.ShapeDtypeStruct((cols * tokens.shape[0], SEQ_MAX), BF),
            jax.ShapeDtypeStruct((cols,) + vectors.shape, F32),
        ],
        scratch_shapes=[
            pltpu.SemaphoreType.DMA((4,)),
            pltpu.SemaphoreType.DMA((2, len(dims))), pltpu.SemaphoreType.DMA((2, len(dims))),
            pltpu.SemaphoreType.DMA((2, cols)), pltpu.SemaphoreType.DMA((2, cols)),
        ],
        compiler_params=pltpu.CompilerParams(collective_id=0, has_side_effects=True),
        name="head",
    )(qk, vo, tokens, vectors)


def attend_forward(qk, v, mask, shards, orders, cotangent):
    cols, _, per_col, _, seq = qk.shape
    heads = cols * per_col
    dims = all_bits()
    levels = len(dims)
    half = shards[0].shape[1] // len(orders)
    pieces = [
        (which, pl.ds(k * half, half), orders[k]) for which in range(len(shards)) for k in range(len(orders))
    ]
    first, second = [0, 1], [2, 3]
    events = [(1, [(p, 0) for p in first]), (5, [(p, 1) for p in first] + [(p, 0) for p in second])]
    events += [(7, [(p, 2) for p in first]), (9, [(p, 1) for p in second] + [(-1, 0)])]
    for step in range(3, levels + 1):
        events.append((-1, [(p, step) for p in first if step < levels] + [(p, step - 1) for p in second]))
    events.append((-1, [(-1, 1)]))
    twos = (2,) * levels
    return pl.pallas_call(
        lambda *refs: attend_forward_kernel(pieces, events, *refs),
        grid=(heads,),
        in_specs=qkv_specs(per_col, seq) + [pl.BlockSpec(a.shape, lambda h: (0, 0)) for a in (*shards, cotangent)],
        out_specs=[head_spec(HEAD_DIM, seq), head_spec(1, seq)] + [pl.BlockSpec(memory_space=pl.ANY)] * (len(shards) + 1),
        out_shape=[
            jax.ShapeDtypeStruct((heads, HEAD_DIM, seq), BF),
            jax.ShapeDtypeStruct((heads, 1, seq), F32),
        ]
        + [jax.ShapeDtypeStruct(twos + a.shape, BF) for a in shards]
        + [jax.ShapeDtypeStruct((cols * cotangent.shape[0], SEQ_MAX), BF)],
        scratch_shapes=[
            pltpu.SemaphoreType.DMA((len(shards) + 1,)),
            pltpu.SemaphoreType.DMA((len(pieces), levels)), pltpu.SemaphoreType.DMA((len(pieces), levels)),
            pltpu.SemaphoreType.DMA((cols,)), pltpu.SemaphoreType.DMA((cols,)),
        ],
        compiler_params=pltpu.CompilerParams(collective_id=2, has_side_effects=True),
        cost_estimate=pl.CostEstimate(
            flops=heads * seq * seq * HEAD_DIM * 16, bytes_accessed=heads * seq * HEAD_DIM * 8,
            transcendentals=heads * seq * seq,
        ),
        name="attend_forward",
    )(qk, qk, v, mask, *shards, cotangent)


def tail_kernel(orders, *refs):
    dims = all_bits()
    levels = len(dims)
    count = len(orders)
    cols, col = lax.axis_size("col"), lax.axis_index("col")
    grads, (token_ref, small_ref) = refs[:count], refs[count : count + 2]
    refs = refs[count + 2 :]
    sums, (out_ref, own_ref) = refs[:count], refs[count : count + 2]
    refs = refs[count + 2 :]
    landed = [refs[i * levels : (i + 1) * levels] for i in range(count)]
    refs = refs[count * levels :]
    (
        token_landed, small_landed, small_sum, block_send, block_recv, col_send, col_recv, small_send, small_recv,
    ) = refs
    feats, seq = token_landed.shape[1], token_landed.shape[2]
    small_bits = axis_bits("row") + axis_bits("dp")
    meet_partners()

    def views(piece, step):
        left = [bit for bit in dims if bit not in orders[piece][:step]]
        axis = left.index(orders[piece][step])
        return grads[piece] if step == 0 else landed[piece][step - 1], axis, my_bit(*orders[piece][step])

    def stage(piece, step):
        operand, axis, mine = views(piece, step)
        return remote(
            operand.at[(slice(None),) * axis + (1 - mine,)], landed[piece][step], block_send.at[piece, step],
            block_recv.at[piece, step], partner(*orders[piece][step]),
        )

    def add(piece, step):
        operand, axis, mine = views(piece, step)
        arrived = landed[piece][step]
        free = levels - 1 - step

        def body(i, carry):
            index = [(i // 2 ** (free - 1 - k)) % 2 for k in range(free)]
            kept = operand[tuple(index[:axis] + [mine] + index[axis:])].astype(F32)
            total = kept + arrived[tuple(index)].astype(F32)
            if free:
                arrived[tuple(index)] = total.astype(BF)
            else:
                sums[piece][...] = total
            return carry

        if free:
            lax.fori_loop(0, 2**free, body, 0)
        else:
            body(0, 0)

    stages = [[stage(piece, step) for step in range(levels)] for piece in range(count)]
    for piece in range(count):
        stages[piece][0].start()
    small_copies = []
    token_copies = []
    for step in range(1, cols):
        to, _ = col_peer(step)
        small_copies.append(
            remote(small_ref.at[to], small_landed.at[step], col_send.at[0, step], col_recv.at[0, step], {"col": to})
        )
        token_copies.append(
            remote(
                token_ref.at[pl.ds(pl.multiple_of(to * feats, 8), feats)], token_landed.at[step],
                col_send.at[1, step], col_recv.at[1, step], {"col": to},
            )
        )
    for copy in small_copies + token_copies:
        copy.start()
    out_ref[:, pl.ds(pl.multiple_of(col * seq, 128), seq)] = token_ref[
        pl.ds(pl.multiple_of(col * feats, 8), feats)
    ].astype(F32)
    for copy in small_copies:
        copy.wait()
    total = small_ref[col]
    for step in range(1, cols):
        total = total + small_landed[step]
    small_sum[0] = total
    for step in range(max(levels, len(small_bits))):
        if step < len(small_bits):
            small_copy = remote(
                small_sum.at[step], small_landed.at[cols + step], small_send.at[step], small_recv.at[step],
                partner(*small_bits[step]),
            )
            small_copy.start()
        for piece in range(count):
            if step < levels:
                stages[piece][step].wait()
                add(piece, step)
                if step + 1 < levels:
                    stages[piece][step + 1].start()
        if step < len(small_bits):
            small_copy.wait()
            small_sum[step + 1] = small_sum[step] + small_landed[cols + step]
    own_ref[...] = small_sum[len(small_bits)]
    for step in range(1, cols):
        _, source = col_peer(step)
        token_copies[step - 1].wait()
        out_ref[:, pl.ds(pl.multiple_of(source * seq, 128), seq)] = token_landed[step].astype(F32)


def tail(orders, grads, token_grad, small):
    dims = all_bits()
    levels = len(dims)
    cols = lax.axis_size("col")
    rows = grads[0].shape[0] * grads[0].shape[1] >> levels
    feats = token_grad.shape[0] // cols
    grads = [g.reshape((2,) * levels + (rows, g.shape[2])) for g in grads]
    widths = [g.shape[-1] for g in grads]
    small_bits = axis_bits("row") + axis_bits("dp")
    vmem = pl.BlockSpec(memory_space=pltpu.VMEM)
    dma = pltpu.SemaphoreType.DMA
    return pl.pallas_call(
        lambda *refs: tail_kernel(orders, *refs),
        in_specs=[vmem] * (len(grads) + 2),
        out_specs=[vmem] * (len(grads) + 2),
        out_shape=[jax.ShapeDtypeStruct((rows, w), F32) for w in widths]
        + [jax.ShapeDtypeStruct((feats, cols * SEQ_MAX), F32), jax.ShapeDtypeStruct(small.shape[1:], F32)],
        scratch_shapes=[
            pltpu.VMEM((2,) * (levels - 1 - step) + (rows, w), BF) for w in widths for step in range(levels)
        ]
        + [
            pltpu.VMEM((cols, feats, SEQ_MAX), BF),
            pltpu.VMEM((cols + len(small_bits),) + small.shape[1:], F32),
            pltpu.VMEM((len(small_bits) + 1,) + small.shape[1:], F32),
            dma((len(grads), levels)), dma((len(grads), levels)), dma((2, cols)), dma((2, cols)),
            dma((len(small_bits),)), dma((len(small_bits),)),
        ],
        compiler_params=pltpu.CompilerParams(collective_id=1, has_side_effects=True),
        name="tail",
    )(*grads, token_grad, small)


def local(
    tokens, w_qkv, bias_qv, w_attn_out, bias_attn_out, w_in, bias_in, w_out, bias_out,
    norm_gains, norm_biases, seq_lengths, seq_offsets, cotangent,
):
    cols = lax.axis_size("col")
    col = lax.axis_index("col")
    rows, _, width = w_qkv.shape
    groups = lax.axis_size("dp") * lax.axis_size("row")
    d = rows * groups
    heads = d // HEAD_DIM
    hid = w_in.shape[1]

    col_bits, row_bits, dp_bits = axis_bits("col"), axis_bits("row"), axis_bits("dp")
    near_first = col_bits[::-1] + row_bits[::-1] + dp_bits
    far_first = col_bits[::-1] + row_bits + dp_bits

    vectors = jnp.concatenate(
        [bias_qv, bias_attn_out[None], bias_out[None], norm_gains, norm_biases, bias_in.reshape(-1, width)], axis=0
    )
    w_flat = w_qkv.reshape(rows, 3 * width)
    w_vo = jnp.concatenate([w_flat[:, 2 * width :], w_attn_out], axis=1)
    full_qk, full_vo, x, vectors = head((near_first, far_first), w_flat[:, : 2 * width], w_vo, tokens, vectors)
    full_qk = full_qk.reshape(cols, d, 2 * width)
    full_vo = full_vo.reshape(cols, d, 2 * width)
    full_v = full_vo[:, :, :width]
    full_attn = full_vo[:, :, width:]
    bias_q, bias_v = vectors[:, 0], vectors[:, 1]
    bias_attn_out, bias_out = vectors[:, 2].reshape(d), vectors[:, 3].reshape(d)
    gains = [vectors[:, 4].reshape(d), vectors[:, 5].reshape(d)]
    shifts = [vectors[:, 6].reshape(d), vectors[:, 7].reshape(d)]
    bias_in = vectors[:, 8:].reshape(cols, hid)

    length = lax.dynamic_index_in_dim(seq_lengths, col, keepdims=False)
    offset = lax.dynamic_index_in_dim(seq_offsets, col, keepdims=False)
    places = lax.broadcasted_iota(jnp.int32, (1, SEQ_MAX), 1)
    live_mask = (places >= offset) & (places < offset + length)
    live = live_mask.astype(F32)
    key_mask = jnp.where(live_mask, 0.0, -1e30).astype(F32)

    def project(weights, shift):
        out = jnp.einsum("cdn,dt->cnt", weights, x, preferred_element_type=F32) + shift[:, :, None]
        return out.astype(BF).reshape(cols, -1, width // HEAD_DIM, HEAD_DIM, SEQ_MAX)

    qk = project(full_qk, jnp.concatenate([bias_q, jnp.zeros_like(bias_q)], axis=1))
    values = project(full_v, bias_v)
    attended, total, full_in, full_out, up = attend_forward(
        qk, values, key_mask, (w_in, w_out), (near_first, far_first), cotangent
    )
    full_in = full_in.reshape(cols, d, hid)
    full_out = full_out.reshape(cols, d, hid)
    attended_cols = attended.reshape(cols, width, SEQ_MAX)
    first_sum = (
        x.astype(F32) + jnp.einsum("cde,cet->dt", full_attn, attended_cols, preferred_element_type=F32)
        + bias_attn_out[:, None]
    )
    normed, xhat1, rstd1 = norm_forward(first_sum, gains[0], shifts[0])
    normed_low = normed.astype(BF)
    hidden = jnp.einsum("cdf,dt->cft", full_in, normed_low, preferred_element_type=F32) + bias_in[:, :, None]
    cdf = 0.5 * (1.0 + lax.erf(hidden * 0.5**0.5))
    active = (hidden * cdf).astype(BF)
    slope = cdf + hidden * jnp.exp(-0.5 * hidden * hidden) * 0.3989422804014327
    second_sum = (
        normed + jnp.einsum("cdf,cft->dt", full_out, active, preferred_element_type=F32) + bias_out[:, None]
    )
    result, xhat2, rstd2 = norm_forward(second_sum, gains[1], shifts[1])
    activations = lax.all_to_all((result * live).astype(BF), "col", split_axis=0, concat_axis=1, tiled=True)

    upstream = up.astype(F32) * live
    gain_two = jnp.sum(upstream * xhat2, axis=1)
    shift_two = jnp.sum(upstream, axis=1)
    d_second = norm_backward(upstream, xhat2, rstd2, gains[1])
    g_bias_out = jnp.sum(d_second, axis=1)
    d_second_low = d_second.astype(BF)
    g_out = jnp.einsum("dt,cft->cdf", d_second_low, active, preferred_element_type=F32)
    d_hidden = jnp.einsum("cdf,dt->cft", full_out, d_second_low, preferred_element_type=F32) * slope
    g_bias_in = jnp.sum(d_hidden, axis=2)
    d_hidden_low = d_hidden.astype(BF)
    g_in = jnp.einsum("dt,cft->cdf", normed_low, d_hidden_low, preferred_element_type=F32)
    g_both = jnp.stack([g_in.astype(BF).reshape(-1, rows, hid), g_out.astype(BF).reshape(-1, rows, hid)], axis=1)
    g_both = lax.psum_scatter(g_both, OWNERS, scatter_dimension=0, tiled=True).astype(F32)
    g_in, g_out = g_both[0, 0], g_both[0, 1]
    d_normed = d_second + jnp.einsum("cdf,cft->dt", full_in, d_hidden_low, preferred_element_type=F32)
    gain_one = jnp.sum(d_normed * xhat1, axis=1)
    shift_one = jnp.sum(d_normed, axis=1)
    d_first = norm_backward(d_normed, xhat1, rstd1, gains[0])
    g_bias_attn = jnp.sum(d_first, axis=1)
    d_first_low = d_first.astype(BF)
    d_attended = jnp.einsum("cde,dt->cet", full_attn, d_first_low, preferred_element_type=F32).astype(BF)
    d_attended = d_attended.reshape(heads, HEAD_DIM, SEQ_MAX)
    d_attended, activations = lax.optimization_barrier((d_attended, activations))
    activations = activations.astype(F32)
    g_attn = jnp.einsum("dt,cet->cde", d_first_low, attended_cols, preferred_element_type=F32)
    d_qk, d_v, bias_sums = attend_backward(qk, values, key_mask, attended, total, d_attended)
    d_qk = d_qk.reshape(cols, 2 * width, SEQ_MAX)
    d_v = d_v.reshape(cols, width, SEQ_MAX)
    bias_sums = jnp.sum(bias_sums, axis=3)
    g_bias_q, g_bias_v = bias_sums[:, 0].reshape(d), bias_sums[:, 1].reshape(d)
    g_qk = jnp.einsum("dt,cnt->cdn", x, d_qk, preferred_element_type=F32)
    g_v = jnp.einsum("dt,cnt->cdn", x, d_v, preferred_element_type=F32)
    token_grad = (
        d_first + jnp.einsum("cdn,cnt->dt", full_qk, d_qk, preferred_element_type=F32)
        + jnp.einsum("cdn,cnt->dt", full_v, d_v, preferred_element_type=F32)
    )
    small = jnp.stack([g_bias_q, g_bias_v, g_bias_attn, g_bias_out, gain_one, gain_two, shift_one, shift_two])
    small = small.reshape(8, cols, width).transpose(1, 0, 2)
    small = jnp.concatenate([small, g_bias_in.reshape(cols, -1, width)], axis=1)
    near = dp_bits + row_bits[::-1] + col_bits
    far = dp_bits + row_bits + col_bits
    g_qk, g_v, g_attn, token_grad, own = tail(
        (near, far, far), [g.astype(BF) for g in (g_qk, g_v, g_attn)], token_grad.astype(BF), small
    )
    return (
        activations, token_grad, jnp.concatenate([g_qk, g_v], axis=1).reshape(rows, 3, width), own[0:2],
        g_attn, own[2], g_in, own[8:].reshape(hid), g_out, own[3], own[4:6], own[6:8],
    )


def solution(mesh):
    return jax.shard_map(
        local,
        mesh=mesh,
        in_specs=(
            P("col", ROWS), P(ROWS, None, "col"), P(None, "col"), P(ROWS, "col"), P("col"),
            P(ROWS, "col"), P("col"), P(ROWS, "col"), P("col"), P(None, "col"), P(None, "col"),
            P(ROWS), P(ROWS), P("col", ROWS),
        ),
        out_specs=(
            P("col", ROWS), P("col", ROWS), P(ROWS, None, "col"), P(None, "col"), P(ROWS, "col"),
            P("col"), P(ROWS, "col"), P("col"), P(ROWS, "col"), P("col"), P(None, "col"), P(None, "col"),
        ),
        check_vma=False,
    )
```

```python
import jax
import jax.numpy as jnp
from jax import lax
from jax.experimental import pallas as pl
from jax.experimental.pallas import tpu as pltpu
from jax.sharding import PartitionSpec as P

HEAD_DIM = 64
SEQ_MAX = 1024
EPSILON = 1e-12
ROWS = ("dp", "row")
ALL = ("dp", "row", "col")
OWNERS = ("col", "dp", "row")
BF = jnp.bfloat16
F32 = jnp.float32
LOG2E = 1.4426950408889634
SCALE = HEAD_DIM ** (-0.5)
QBLOCK = 256
EXTRA = 16
GRAD_ROWS = 256


def dot_nn(a, b):
    return lax.dot_general(a, b, (((1,), (0,)), ((), ())), preferred_element_type=F32)


def dot_tn(a, b):
    return lax.dot_general(a, b, (((0,), (0,)), ((), ())), preferred_element_type=F32)


def dot_nt(a, b):
    return lax.dot_general(a, b, (((1,), (1,)), ((), ())), preferred_element_type=F32)


def mean_rows(v):
    return jnp.mean(v, axis=0, keepdims=True)


def norm_forward(values, gain, shift):
    centred = values - mean_rows(values)
    inverse = lax.rsqrt(mean_rows(centred * centred) + EPSILON)
    scaled = centred * inverse
    return scaled * gain[:, None] + shift[:, None], scaled, inverse


def norm_backward(upstream, scaled, inverse, gain):
    weighted = upstream * gain[:, None]
    return inverse * (weighted - mean_rows(weighted) - scaled * mean_rows(weighted * scaled))


def stack_rows(rows, width):
    place = lax.broadcasted_iota(jnp.int32, (EXTRA, width), 0)
    out = jnp.zeros((EXTRA, width), F32)
    for i, row in enumerate(rows):
        out = jnp.where(place == i, row, out)
    return out.astype(BF)


def three_parts(row):
    high = row.astype(BF).astype(F32)
    middle = (row - high).astype(BF).astype(F32)
    return high, middle, row - high - middle


def projection_spec(first, count, per_col, seq):
    return pl.BlockSpec((1, count, 1, HEAD_DIM, seq), lambda h: (h // per_col, first, h % per_col, 0, 0))


def head_spec(rows, seq):
    return pl.BlockSpec((1, rows, seq), lambda h: (h, 0, 0))


def qkv_specs(per_col, seq):
    return [
        projection_spec(0, 1, per_col, seq), projection_spec(1, 1, per_col, seq), projection_spec(0, 1, per_col, seq),
        pl.BlockSpec((1, seq), lambda h: (0, 0)),
    ]


def axis_bits(name):
    size = lax.axis_size(name)
    return [(name, 1 << b) for b in reversed(range(size.bit_length() - 1))]


def my_bit(name, bit):
    return (lax.axis_index(name) // bit) % 2


def partner(name, bit):
    return {name: lax.axis_index(name) + bit * (1 - 2 * my_bit(name, bit))}


def all_bits():
    return axis_bits("col") + axis_bits("dp") + axis_bits("row")


def col_peer(step):
    cols = lax.axis_size("col")
    col = lax.axis_index("col")
    return (col + step) % cols, (col + cols - step) % cols


def remote(src, dst, send, recv, device):
    return pltpu.make_async_remote_copy(
        src_ref=src, dst_ref=dst, send_sem=send, recv_sem=recv, device_id=device,
        device_id_type=pl.DeviceIdType.MESH,
    )


def meet_partners():
    barrier = pltpu.get_barrier_semaphore()
    devices = [partner(name, bit) for name, bit in axis_bits("dp") + axis_bits("row")]
    devices += [{"col": col_peer(step)[0]} for step in range(1, lax.axis_size("col"))]
    for device in devices:
        pl.semaphore_signal(barrier, inc=1, device_id=device, device_id_type=pl.DeviceIdType.MESH)
    pl.semaphore_wait(barrier, len(devices))


def attend_forward_kernel(
    pieces, events, q_ref, k_ref, v_ref, mask_ref, *refs
):
    count = 1 + max(which for which, _, _ in pieces)
    shards, cotangent_ref, refs = refs[:count], refs[count], refs[count + 1 :]
    (out_ref, total_ref), fulls, up_ref = refs[:2], refs[2 : count + 2], refs[count + 2]
    own_sem, block_send, block_recv, col_send, col_recv = refs[count + 3 :]
    group, col = lax.axis_size("col"), lax.axis_index("col")
    feats, window = cotangent_ref.shape[0], up_ref.shape[1]
    dims = all_bits()
    levels = len(dims)
    head = pl.program_id(0)
    place = [my_bit(name, bit) for name, bit in dims]

    def stage(piece, step):
        which, cols, order = pieces[piece]
        index = tuple(slice(None) if bit in order[:step] else at for bit, at in zip(dims, place))
        target = fulls[which].at[index + (slice(None), cols)]
        return remote(
            shards[which].at[:, cols] if step == 0 else target, target, block_send.at[piece, step],
            block_recv.at[piece, step], partner(*order[step]),
        )

    def own(which):
        return pltpu.make_async_copy(shards[which], fulls[which].at[tuple(place)], own_sem.at[which])

    def transpose(step):
        to, _ = col_peer(step)
        src = cotangent_ref.at[:, pl.ds(pl.multiple_of(to * window, 128), window)]
        dst = up_ref.at[pl.ds(pl.multiple_of(col * feats, 8), feats)]
        if step == 0:
            return pltpu.make_async_copy(src, dst, own_sem.at[count])
        return remote(src, dst, col_send.at[step], col_recv.at[step], {"col": to})

    def advance(piece, step):
        if piece < 0:
            for k in range(1, group):
                transpose(k).start() if step == 0 else transpose(k).wait()
            return
        stage(piece, step).wait()
        if step + 1 < levels:
            stage(piece, step + 1).start()

    @pl.when(head == 0)
    def _():
        for which in range(count):
            own(which).start()
        transpose(0).start()
        meet_partners()
        for piece in range(len(pieces)):
            stage(piece, 0).start()
        for which in range(count):
            own(which).wait()
        transpose(0).wait()

    for at, moves in events:
        if at >= 0:

            @pl.when(head == at)
            def _(moves=moves):
                for piece, step in moves:
                    advance(piece, step)

    seq = q_ref.shape[-1]
    one = jnp.ones((1, seq), F32)
    keys = jnp.concatenate([k_ref[0, 0, 0], stack_rows([mask_ref[...]], seq)], axis=0).T
    queries = jnp.concatenate([q_ref[0, 0, 0], stack_rows([one], seq)], axis=0)
    values = v_ref[0, 0, 0]
    for j in range(seq // QBLOCK):
        cols = slice(j * QBLOCK, (j + 1) * QBLOCK)
        scores = dot_nn(keys, queries[:, cols])
        largest = jnp.max(scores, axis=0, keepdims=True)
        exponent = jnp.exp2((scores - largest) * (SCALE * LOG2E))
        total = jnp.sum(exponent, axis=0, keepdims=True)
        weights = (exponent * (1.0 / total)).astype(BF)
        out_ref[0, :, cols] = dot_nn(values, weights).astype(BF)
        total_ref[0, :, cols] = largest + jnp.log(total) * (1.0 / SCALE)

    @pl.when(head == pl.num_programs(0) - 1)
    def _():
        for at, moves in events:
            if at < 0:
                for piece, step in moves:
                    advance(piece, step)


def attend_backward_kernel(
    pieces, events, per_col, q_ref, k_ref, v_ref, mask_ref, out_ref, total_ref, up_ref, x_ref, w_qk_ref, w_vo_ref,
    first_ref, *refs
):
    dims = all_bits()
    levels = len(dims)
    count = 1 + max(which for which, _, _ in pieces)
    grads, refs = refs[:count], refs[count:]
    (g_qk_ref, g_v_ref, g_out_ref, token_ref, bias_ref), refs = refs[:5], refs[5:]
    sums, refs = refs[:count], refs[count:]
    (dk_ref, dv_ref, all_qk_ref, all_v_ref, all_out_ref, token_sum_ref), refs = refs[:6], refs[6:]
    kept, refs = refs[: len(pieces)], refs[len(pieces) :]
    landed = [refs[i * levels : (i + 1) * levels] for i in range(len(pieces))]
    keep_sem, block_send, block_recv = refs[len(pieces) * levels :]
    seq = q_ref.shape[-1]
    head = pl.program_id(0)
    local_head = head % per_col

    def views(piece, step):
        order = pieces[piece][2]
        left = [bit for bit in dims if bit not in order[:step]]
        return left.index(order[step]), my_bit(*order[step])

    def source(piece, axis, at):
        which, lanes, _ = pieces[piece]
        return grads[which].at[(slice(None),) * axis + (at,) + (slice(None),) * (levels - axis) + (lanes,)]

    def keep(piece):
        axis, mine = views(piece, 0)
        return pltpu.make_async_copy(source(piece, axis, mine), kept[piece], keep_sem.at[piece])

    def stage(piece, step):
        axis, mine = views(piece, step)
        if step == 0:
            src = source(piece, axis, 1 - mine)
        else:
            src = landed[piece][step - 1].at[(slice(None),) * axis + (1 - mine,)]
        return remote(
            src, landed[piece][step], block_send.at[piece, step], block_recv.at[piece, step],
            partner(*pieces[piece][2][step]),
        )

    def advance(piece, step):
        if step < 0:
            stage(piece, 0).start()
            return
        axis, mine = views(piece, step)
        which, lanes, _ = pieces[piece]
        arrived = landed[piece][step]
        free = levels - 1 - step
        if step == 0:
            keep(piece).wait()
        stage(piece, step).wait()

        def body(i, carry):
            index = [(i // 2 ** (free - 1 - k)) % 2 for k in range(free)]
            if step == 0:
                mine_value = kept[piece][tuple(index)]
            else:
                mine_value = landed[piece][step - 1][tuple(index[:axis] + [mine] + index[axis:])]
            total = mine_value.astype(F32) + arrived[tuple(index)].astype(F32)
            if free:
                arrived[tuple(index)] = total.astype(BF)
            else:
                sums[which][:, lanes] = total
            return carry

        if free:
            lax.fori_loop(0, 2**free, body, 0)
        else:
            body(0, 0)
        if step + 1 < levels:
            stage(piece, step + 1).start()

    @pl.when(head == 0)
    def _():
        for piece in range(len(pieces)):
            keep(piece).start()
        meet_partners()
        token_sum_ref[...] = first_ref[...]

    for at, moves in events:
        if at >= 0:

            @pl.when(head == at)
            def _(moves=moves):
                for piece, step in moves:
                    advance(piece, step)

    one = jnp.ones((1, seq), F32)
    keys = k_ref[0, 0, 0]
    queries = q_ref[0, 0, 0]
    up = up_ref[0]
    delta = jnp.sum(up.astype(F32) * out_ref[0].astype(F32), axis=0, keepdims=True)
    key_side = jnp.concatenate([keys, stack_rows([mask_ref[...], one, one, one], seq)], axis=0).T
    value_side = jnp.concatenate([v_ref[0, 0, 0], stack_rows([one, one, one], seq)], axis=0).T
    query_side = jnp.concatenate([queries, stack_rows([one, *three_parts(-total_ref[0])], seq)], axis=0)
    up_side = jnp.concatenate([up, stack_rows(three_parts(-delta), seq)], axis=0)
    lanes = 128
    my_rows = pl.ds(pl.multiple_of(local_head * HEAD_DIM, HEAD_DIM), HEAD_DIM)
    key_rows = pl.ds(pl.multiple_of((per_col + local_head) * HEAD_DIM, HEAD_DIM), HEAD_DIM)
    sum_q = jnp.zeros((HEAD_DIM, lanes), F32)
    for j in range(seq // QBLOCK):
        cols = slice(j * QBLOCK, (j + 1) * QBLOCK)
        weights = jnp.exp2(dot_nn(key_side, query_side[:, cols]) * (SCALE * LOG2E))
        d_scores = (weights * dot_nn(value_side, up_side[:, cols])).astype(BF)
        d_q = dot_nn(keys, d_scores) * SCALE
        for part in range(QBLOCK // lanes):
            sum_q += d_q[:, part * lanes : (part + 1) * lanes]
        all_qk_ref[my_rows, cols] = d_q.astype(BF)
        d_k = dot_nt(queries[:, cols], d_scores)
        d_v = dot_nt(up[:, cols], weights.astype(BF))
        if j == 0:
            dk_ref[...] = d_k
            dv_ref[...] = d_v
        else:
            dk_ref[...] += d_k
            dv_ref[...] += d_v
    all_qk_ref[key_rows] = (dk_ref[...] * SCALE).astype(BF)
    all_v_ref[my_rows] = dv_ref[...].astype(BF)
    all_out_ref[my_rows] = out_ref[0]
    bias_ref[0, 0] = sum_q
    sum_v = jnp.zeros((HEAD_DIM, lanes), F32)
    for part in range(seq // lanes):
        sum_v += dv_ref[:, part * lanes : (part + 1) * lanes]
    bias_ref[0, 1] = sum_v

    @pl.when(local_head == per_col - 1)
    def _():
        width = all_v_ref.shape[0]

        def body(i, carry):
            rows = pl.ds(pl.multiple_of(i * GRAD_ROWS, GRAD_ROWS), GRAD_ROWS)
            x = x_ref[rows]
            g_qk_ref[0, rows] = dot_nt(x, all_qk_ref[...]).astype(BF)
            g_v_ref[0, rows] = dot_nt(x, all_v_ref[...]).astype(BF)
            g_out_ref[0, rows] = dot_nt(first_ref[rows].astype(BF), all_out_ref[...]).astype(BF)
            token = (
                token_sum_ref[rows] + dot_nn(w_qk_ref[0, rows], all_qk_ref[...])
                + dot_nn(w_vo_ref[0, rows, :width], all_v_ref[...])
            )
            token_sum_ref[rows] = token
            token_ref[rows] = token.astype(BF)
            return carry

        lax.fori_loop(0, x_ref.shape[0] // GRAD_ROWS, body, 0)

    @pl.when(head == pl.num_programs(0) - 1)
    def _():
        for at, moves in events:
            if at < 0:
                for piece, step in moves:
                    advance(piece, step)


def outer_kernel(a_ref, b_ref, out_ref):
    def body(i, carry):
        rows = pl.ds(pl.multiple_of(i * GRAD_ROWS, GRAD_ROWS), GRAD_ROWS)
        out_ref[0, rows] = dot_nt(a_ref[rows], b_ref[0]).astype(BF)
        return carry

    lax.fori_loop(0, a_ref.shape[0] // GRAD_ROWS, body, 0)


def outer(a, b):
    cols, n, seq = b.shape
    d = a.shape[0]
    return pl.pallas_call(
        outer_kernel,
        grid=(cols,),
        in_specs=[pl.BlockSpec((d, seq), lambda c: (0, 0)), pl.BlockSpec((1, n, seq), lambda c: (c, 0, 0))],
        out_specs=pl.BlockSpec((1, d, n), lambda c: (c, 0, 0)),
        out_shape=jax.ShapeDtypeStruct((cols, d, n), BF),
        cost_estimate=pl.CostEstimate(
            flops=2 * cols * d * n * seq, bytes_accessed=2 * (d * seq + b.size + cols * d * n), transcendentals=0
        ),
        name="outer",
    )(a, b)


def head_kernel(
    orders, qk_ref, vo_ref, tokens_ref, vectors_ref, full_qk_ref, full_vo_ref, x_ref, all_vectors_ref,
    own_sem, block_send, block_recv, col_send, col_recv,
):
    dims = all_bits()
    cols, col = lax.axis_size("col"), lax.axis_index("col")
    feats, seq = tokens_ref.shape[0], x_ref.shape[1]
    place = [my_bit(name, bit) for name, bit in dims]
    pieces = [(qk_ref, full_qk_ref), (vo_ref, full_vo_ref)]
    my_feats = pl.ds(pl.multiple_of(col * feats, 8), feats)
    own = [pltpu.make_async_copy(src, dst.at[tuple(place)], own_sem.at[i]) for i, (src, dst) in enumerate(pieces)]
    own.append(
        pltpu.make_async_copy(
            tokens_ref.at[:, pl.ds(pl.multiple_of(col * seq, 128), seq)], x_ref.at[my_feats], own_sem.at[2]
        )
    )
    own.append(pltpu.make_async_copy(vectors_ref, all_vectors_ref.at[col], own_sem.at[3]))
    for copy in own:
        copy.start()
    meet_partners()

    def stage(piece, step):
        src, full = pieces[piece]
        done = orders[piece][:step]
        index = tuple(slice(None) if bit in done else at for bit, at in zip(dims, place))
        return remote(
            src if step == 0 else full.at[index], full.at[index], block_send.at[piece, step],
            block_recv.at[piece, step], partner(*orders[piece][step]),
        )

    stages = [[stage(piece, step) for step in range(len(dims))] for piece in range(2)]
    for piece in range(2):
        stages[piece][0].start()
    transposes = []
    for step in range(1, cols):
        to, _ = col_peer(step)
        transposes.append(
            remote(vectors_ref, all_vectors_ref.at[col], col_send.at[0, step], col_recv.at[0, step], {"col": to})
        )
        transposes.append(
            remote(
                tokens_ref.at[:, pl.ds(pl.multiple_of(to * seq, 128), seq)], x_ref.at[my_feats],
                col_send.at[1, step], col_recv.at[1, step], {"col": to},
            )
        )
    for copy in transposes[::2]:
        copy.start()
    for copy in own:
        copy.wait()
    for step in range(len(dims)):
        for piece in range(2):
            stages[piece][step].wait()
            if step + 1 < len(dims):
                stages[piece][step + 1].start()
        if step + 1 == len(axis_bits("col")):
            for copy in transposes[1::2]:
                copy.start()
    for copy in transposes:
        copy.wait()


def head(orders, qk, vo, tokens, vectors):
    dims = all_bits()
    cols = lax.axis_size("col")
    twos = (2,) * len(dims)
    vmem = pl.BlockSpec(memory_space=pltpu.VMEM)
    return pl.pallas_call(
        lambda *refs: head_kernel(orders, *refs),
        in_specs=[vmem] * 4,
        out_specs=[vmem] * 4,
        out_shape=[
            jax.ShapeDtypeStruct(twos + qk.shape, BF),
            jax.ShapeDtypeStruct(twos + vo.shape, BF),
            jax.ShapeDtypeStruct((cols * tokens.shape[0], SEQ_MAX), BF),
            jax.ShapeDtypeStruct((cols,) + vectors.shape, F32),
        ],
        scratch_shapes=[
            pltpu.SemaphoreType.DMA((4,)),
            pltpu.SemaphoreType.DMA((2, len(dims))), pltpu.SemaphoreType.DMA((2, len(dims))),
            pltpu.SemaphoreType.DMA((2, cols)), pltpu.SemaphoreType.DMA((2, cols)),
        ],
        compiler_params=pltpu.CompilerParams(collective_id=0, has_side_effects=True),
        name="head",
    )(qk, vo, tokens, vectors)


def attend_forward(qk, v, mask, shards, orders, cotangent):
    cols, _, per_col, _, seq = qk.shape
    heads = cols * per_col
    dims = all_bits()
    levels = len(dims)
    half = shards[0].shape[1] // len(orders)
    pieces = [
        (which, pl.ds(k * half, half), orders[k]) for which in range(len(shards)) for k in range(len(orders))
    ]
    first, second = [0, 1], [2, 3]
    events = [(1, [(p, 0) for p in first]), (5, [(p, 1) for p in first] + [(p, 0) for p in second])]
    events += [(7, [(p, 2) for p in first]), (9, [(p, 1) for p in second] + [(-1, 0)])]
    for step in range(3, levels + 1):
        events.append((-1, [(p, step) for p in first if step < levels] + [(p, step - 1) for p in second]))
    events.append((-1, [(-1, 1)]))
    twos = (2,) * levels
    return pl.pallas_call(
        lambda *refs: attend_forward_kernel(pieces, events, *refs),
        grid=(heads,),
        in_specs=qkv_specs(per_col, seq) + [pl.BlockSpec(a.shape, lambda h: (0, 0)) for a in (*shards, cotangent)],
        out_specs=[head_spec(HEAD_DIM, seq), head_spec(1, seq)] + [pl.BlockSpec(memory_space=pl.ANY)] * (len(shards) + 1),
        out_shape=[
            jax.ShapeDtypeStruct((heads, HEAD_DIM, seq), BF),
            jax.ShapeDtypeStruct((heads, 1, seq), F32),
        ]
        + [jax.ShapeDtypeStruct(twos + a.shape, BF) for a in shards]
        + [jax.ShapeDtypeStruct((cols * cotangent.shape[0], SEQ_MAX), BF)],
        scratch_shapes=[
            pltpu.SemaphoreType.DMA((len(shards) + 1,)),
            pltpu.SemaphoreType.DMA((len(pieces), levels)), pltpu.SemaphoreType.DMA((len(pieces), levels)),
            pltpu.SemaphoreType.DMA((cols,)), pltpu.SemaphoreType.DMA((cols,)),
        ],
        compiler_params=pltpu.CompilerParams(collective_id=2, has_side_effects=True),
        cost_estimate=pl.CostEstimate(
            flops=heads * seq * seq * HEAD_DIM * 16, bytes_accessed=heads * seq * HEAD_DIM * 8,
            transcendentals=heads * seq * seq,
        ),
        name="attend_forward",
    )(qk, qk, v, mask, *shards, cotangent)


def attend_backward(qk, v, mask, attended, total, d_attended, x, w_qk, w_vo, d_first, grads, orders):
    cols, _, per_col, _, seq = qk.shape
    heads = cols * per_col
    dims = all_bits()
    levels = len(dims)
    d, width = x.shape[0], per_col * HEAD_DIM
    rows = d * cols >> levels
    half = grads[0].shape[2] // len(orders)
    grads = [g.reshape((2,) * levels + (rows, g.shape[2])) for g in grads]
    pieces = [(which, pl.ds(k * half, half), orders[k]) for which in range(len(grads)) for k in range(len(orders))]
    first, second = [0, 1], [2, 3]
    events = [(0, [(p, -1) for p in first]), (2, [(p, 0) for p in first] + [(p, -1) for p in second])]
    events += [(4, [(p, 0) for p in second]), (6, [(p, 1) for p in first])]
    events += [(9, [(p, 2) for p in first] + [(p, 1) for p in second]), (11, [(p, 2) for p in second])]
    events += [(-1, [(p, step) for p in first + second]) for step in range(3, levels)]

    def whole(a):
        return pl.BlockSpec(a.shape, lambda h: (0,) * len(a.shape))

    def column_spec(n):
        return pl.BlockSpec((1, d, n), lambda h: (h // per_col, 0, 0))

    token = jax.ShapeDtypeStruct((d, seq), BF)
    summed = [jax.ShapeDtypeStruct((rows, g.shape[-1]), F32) for g in grads]
    dma = pltpu.SemaphoreType.DMA
    return pl.pallas_call(
        lambda *refs: attend_backward_kernel(pieces, events, per_col, *refs),
        grid=(heads,),
        in_specs=qkv_specs(per_col, seq)
        + [head_spec(HEAD_DIM, seq), head_spec(1, seq), head_spec(HEAD_DIM, seq)]
        + [whole(x), column_spec(2 * width), column_spec(2 * width), whole(d_first)]
        + [pl.BlockSpec(memory_space=pl.ANY)] * len(grads),
        out_specs=[column_spec(2 * width), column_spec(width), column_spec(width), whole(token)]
        + [pl.BlockSpec((1, 2, HEAD_DIM, 128), lambda h: (h, 0, 0, 0))]
        + [whole(a) for a in summed],
        out_shape=[
            jax.ShapeDtypeStruct((cols, d, 2 * width), BF),
            jax.ShapeDtypeStruct((cols, d, width), BF),
            jax.ShapeDtypeStruct((cols, d, width), BF),
            token,
            jax.ShapeDtypeStruct((heads, 2, HEAD_DIM, 128), F32),
        ]
        + summed,
        scratch_shapes=[
            pltpu.VMEM((HEAD_DIM, seq), F32), pltpu.VMEM((HEAD_DIM, seq), F32),
            pltpu.VMEM((2 * width, seq), BF), pltpu.VMEM((width, seq), BF), pltpu.VMEM((width, seq), BF),
            pltpu.VMEM((d, seq), F32),
        ]
        + [pltpu.VMEM((2,) * (levels - 1) + (rows, half), BF) for _ in pieces]
        + [pltpu.VMEM((2,) * (levels - 1 - step) + (rows, half), BF) for _ in pieces for step in range(levels)]
        + [dma((len(pieces),)), dma((len(pieces), levels)), dma((len(pieces), levels))],
        compiler_params=pltpu.CompilerParams(collective_id=3, has_side_effects=True),
        cost_estimate=pl.CostEstimate(
            flops=heads * seq * seq * HEAD_DIM * 40, bytes_accessed=heads * seq * HEAD_DIM * 16,
            transcendentals=heads * seq * seq,
        ),
        name="attend_backward",
    )(qk, qk, v, mask, attended, total, d_attended, x, w_qk, w_vo, d_first, *grads)


def tail_kernel(orders, *refs):
    dims = all_bits()
    levels = len(dims)
    count = len(orders)
    cols, col = lax.axis_size("col"), lax.axis_index("col")
    grads, (token_ref, small_ref) = refs[:count], refs[count : count + 2]
    refs = refs[count + 2 :]
    sums, (out_ref, own_ref) = refs[:count], refs[count : count + 2]
    refs = refs[count + 2 :]
    landed = [refs[i * levels : (i + 1) * levels] for i in range(count)]
    refs = refs[count * levels :]
    (
        token_landed, small_landed, small_sum, block_send, block_recv, col_send, col_recv, small_send, small_recv,
    ) = refs
    feats, seq = token_landed.shape[1], token_landed.shape[2]
    small_bits = axis_bits("row") + axis_bits("dp")
    meet_partners()

    def views(piece, step):
        left = [bit for bit in dims if bit not in orders[piece][:step]]
        axis = left.index(orders[piece][step])
        return grads[piece] if step == 0 else landed[piece][step - 1], axis, my_bit(*orders[piece][step])

    def stage(piece, step):
        operand, axis, mine = views(piece, step)
        return remote(
            operand.at[(slice(None),) * axis + (1 - mine,)], landed[piece][step], block_send.at[piece, step],
            block_recv.at[piece, step], partner(*orders[piece][step]),
        )

    def add(piece, step):
        operand, axis, mine = views(piece, step)
        arrived = landed[piece][step]
        free = levels - 1 - step

        def body(i, carry):
            index = [(i // 2 ** (free - 1 - k)) % 2 for k in range(free)]
            kept = operand[tuple(index[:axis] + [mine] + index[axis:])].astype(F32)
            total = kept + arrived[tuple(index)].astype(F32)
            if free:
                arrived[tuple(index)] = total.astype(BF)
            else:
                sums[piece][...] = total
            return carry

        if free:
            lax.fori_loop(0, 2**free, body, 0)
        else:
            body(0, 0)

    stages = [[stage(piece, step) for step in range(levels)] for piece in range(count)]
    for piece in range(count):
        stages[piece][0].start()
    small_copies = []
    token_copies = []
    for step in range(1, cols):
        to, _ = col_peer(step)
        small_copies.append(
            remote(small_ref.at[to], small_landed.at[step], col_send.at[0, step], col_recv.at[0, step], {"col": to})
        )
        token_copies.append(
            remote(
                token_ref.at[pl.ds(pl.multiple_of(to * feats, 8), feats)], token_landed.at[step],
                col_send.at[1, step], col_recv.at[1, step], {"col": to},
            )
        )
    for copy in small_copies + token_copies:
        copy.start()
    out_ref[:, pl.ds(pl.multiple_of(col * seq, 128), seq)] = token_ref[
        pl.ds(pl.multiple_of(col * feats, 8), feats)
    ].astype(F32)
    for copy in small_copies:
        copy.wait()
    total = small_ref[col]
    for step in range(1, cols):
        total = total + small_landed[step]
    small_sum[0] = total
    for step in range(max(levels, len(small_bits))):
        if step < len(small_bits):
            small_copy = remote(
                small_sum.at[step], small_landed.at[cols + step], small_send.at[step], small_recv.at[step],
                partner(*small_bits[step]),
            )
            small_copy.start()
        for piece in range(count):
            if step < levels:
                stages[piece][step].wait()
                add(piece, step)
                if step + 1 < levels:
                    stages[piece][step + 1].start()
        if step < len(small_bits):
            small_copy.wait()
            small_sum[step + 1] = small_sum[step] + small_landed[cols + step]
    own_ref[...] = small_sum[len(small_bits)]
    for step in range(1, cols):
        _, source = col_peer(step)
        token_copies[step - 1].wait()
        out_ref[:, pl.ds(pl.multiple_of(source * seq, 128), seq)] = token_landed[step].astype(F32)


def tail(orders, grads, token_grad, small):
    dims = all_bits()
    levels = len(dims)
    cols = lax.axis_size("col")
    rows = grads[0].shape[0] * grads[0].shape[1] >> levels
    feats = token_grad.shape[0] // cols
    grads = [g.reshape((2,) * levels + (rows, g.shape[2])) for g in grads]
    widths = [g.shape[-1] for g in grads]
    small_bits = axis_bits("row") + axis_bits("dp")
    vmem = pl.BlockSpec(memory_space=pltpu.VMEM)
    dma = pltpu.SemaphoreType.DMA
    return pl.pallas_call(
        lambda *refs: tail_kernel(orders, *refs),
        in_specs=[vmem] * (len(grads) + 2),
        out_specs=[vmem] * (len(grads) + 2),
        out_shape=[jax.ShapeDtypeStruct((rows, w), F32) for w in widths]
        + [jax.ShapeDtypeStruct((feats, cols * SEQ_MAX), F32), jax.ShapeDtypeStruct(small.shape[1:], F32)],
        scratch_shapes=[
            pltpu.VMEM((2,) * (levels - 1 - step) + (rows, w), BF) for w in widths for step in range(levels)
        ]
        + [
            pltpu.VMEM((cols, feats, SEQ_MAX), BF),
            pltpu.VMEM((cols + len(small_bits),) + small.shape[1:], F32),
            pltpu.VMEM((len(small_bits) + 1,) + small.shape[1:], F32),
            dma((len(grads), levels)), dma((len(grads), levels)), dma((2, cols)), dma((2, cols)),
            dma((len(small_bits),)), dma((len(small_bits),)),
        ],
        compiler_params=pltpu.CompilerParams(collective_id=1, has_side_effects=True),
        name="tail",
    )(*grads, token_grad, small)


def local(
    tokens, w_qkv, bias_qv, w_attn_out, bias_attn_out, w_in, bias_in, w_out, bias_out,
    norm_gains, norm_biases, seq_lengths, seq_offsets, cotangent,
):
    cols = lax.axis_size("col")
    col = lax.axis_index("col")
    rows, _, width = w_qkv.shape
    groups = lax.axis_size("dp") * lax.axis_size("row")
    d = rows * groups
    heads = d // HEAD_DIM
    hid = w_in.shape[1]

    col_bits, row_bits, dp_bits = axis_bits("col"), axis_bits("row"), axis_bits("dp")
    near_first = col_bits[::-1] + row_bits[::-1] + dp_bits
    far_first = col_bits[::-1] + row_bits + dp_bits

    vectors = jnp.concatenate(
        [bias_qv, bias_attn_out[None], bias_out[None], norm_gains, norm_biases, bias_in.reshape(-1, width)], axis=0
    )
    w_flat = w_qkv.reshape(rows, 3 * width)
    w_vo = jnp.concatenate([w_flat[:, 2 * width :], w_attn_out], axis=1)
    full_qk, full_vo, x, vectors = head((near_first, far_first), w_flat[:, : 2 * width], w_vo, tokens, vectors)
    full_qk = full_qk.reshape(cols, d, 2 * width)
    full_vo = full_vo.reshape(cols, d, 2 * width)
    full_v = full_vo[:, :, :width]
    full_attn = full_vo[:, :, width:]
    bias_q, bias_v = vectors[:, 0], vectors[:, 1]
    bias_attn_out, bias_out = vectors[:, 2].reshape(d), vectors[:, 3].reshape(d)
    gains = [vectors[:, 4].reshape(d), vectors[:, 5].reshape(d)]
    shifts = [vectors[:, 6].reshape(d), vectors[:, 7].reshape(d)]
    bias_in = vectors[:, 8:].reshape(cols, hid)

    length = lax.dynamic_index_in_dim(seq_lengths, col, keepdims=False)
    offset = lax.dynamic_index_in_dim(seq_offsets, col, keepdims=False)
    places = lax.broadcasted_iota(jnp.int32, (1, SEQ_MAX), 1)
    live_mask = (places >= offset) & (places < offset + length)
    live = live_mask.astype(F32)
    key_mask = jnp.where(live_mask, 0.0, -1e30).astype(F32)

    def project(weights, shift):
        out = jnp.einsum("cdn,dt->cnt", weights, x, preferred_element_type=F32) + shift[:, :, None]
        return out.astype(BF).reshape(cols, -1, width // HEAD_DIM, HEAD_DIM, SEQ_MAX)

    qk = project(full_qk, jnp.concatenate([bias_q, jnp.zeros_like(bias_q)], axis=1))
    values = project(full_v, bias_v)
    attended, total, full_in, full_out, up = attend_forward(
        qk, values, key_mask, (w_in, w_out), (near_first, far_first), cotangent
    )
    full_in = full_in.reshape(cols, d, hid)
    full_out = full_out.reshape(cols, d, hid)
    attended_cols = attended.reshape(cols, width, SEQ_MAX)
    first_sum = (
        x.astype(F32) + jnp.einsum("cde,cet->dt", full_attn, attended_cols, preferred_element_type=F32)
        + bias_attn_out[:, None]
    )
    normed, xhat1, rstd1 = norm_forward(first_sum, gains[0], shifts[0])
    normed_low = normed.astype(BF)
    hidden = jnp.einsum("cdf,dt->cft", full_in, normed_low, preferred_element_type=F32) + bias_in[:, :, None]
    cdf = 0.5 * (1.0 + lax.erf(hidden * 0.5**0.5))
    active = (hidden * cdf).astype(BF)
    slope = cdf + hidden * jnp.exp(-0.5 * hidden * hidden) * 0.3989422804014327
    second_sum = (
        normed + jnp.einsum("cdf,cft->dt", full_out, active, preferred_element_type=F32) + bias_out[:, None]
    )
    result, xhat2, rstd2 = norm_forward(second_sum, gains[1], shifts[1])
    activations = lax.all_to_all((result * live).astype(BF), "col", split_axis=0, concat_axis=1, tiled=True)

    upstream = up.astype(F32) * live
    gain_two = jnp.sum(upstream * xhat2, axis=1)
    shift_two = jnp.sum(upstream, axis=1)
    d_second = norm_backward(upstream, xhat2, rstd2, gains[1])
    g_bias_out = jnp.sum(d_second, axis=1)
    d_second_low = d_second.astype(BF)
    g_out = outer(d_second_low, active)
    d_hidden = jnp.einsum("cdf,dt->cft", full_out, d_second_low, preferred_element_type=F32) * slope
    g_bias_in = jnp.sum(d_hidden, axis=2)
    d_hidden_low = d_hidden.astype(BF)
    g_in = outer(normed_low, d_hidden_low)
    d_normed = d_second + jnp.einsum("cdf,cft->dt", full_in, d_hidden_low, preferred_element_type=F32)
    gain_one = jnp.sum(d_normed * xhat1, axis=1)
    shift_one = jnp.sum(d_normed, axis=1)
    d_first = norm_backward(d_normed, xhat1, rstd1, gains[0])
    g_bias_attn = jnp.sum(d_first, axis=1)
    d_first_low = d_first.astype(BF)
    d_attended = jnp.einsum("cde,dt->cet", full_attn, d_first_low, preferred_element_type=F32).astype(BF)
    d_attended = d_attended.reshape(heads, HEAD_DIM, SEQ_MAX)
    d_attended, activations = lax.optimization_barrier((d_attended, activations))
    activations = activations.astype(F32)
    near = dp_bits + row_bits[::-1] + col_bits
    far = dp_bits + row_bits + col_bits
    g_qk, g_v, g_attn, token_grad, bias_sums, g_out, g_in = attend_backward(
        qk, values, key_mask, attended, total, d_attended, x, full_qk, full_vo, d_first, (g_out, g_in), (near, far)
    )
    bias_sums = jnp.sum(bias_sums, axis=3)
    g_bias_q, g_bias_v = bias_sums[:, 0].reshape(d), bias_sums[:, 1].reshape(d)

    small = jnp.stack([g_bias_q, g_bias_v, g_bias_attn, g_bias_out, gain_one, gain_two, shift_one, shift_two])
    small = small.reshape(8, cols, width).transpose(1, 0, 2)
    small = jnp.concatenate([small, g_bias_in.reshape(cols, -1, width)], axis=1)
    g_qk, g_v, g_attn, token_grad, own = tail((near, far, far), (g_qk, g_v, g_attn), token_grad, small)
    return (
        activations, token_grad, jnp.concatenate([g_qk, g_v], axis=1).reshape(rows, 3, width), own[0:2],
        g_attn, own[2], g_in, own[8:].reshape(hid), g_out, own[3], own[4:6], own[6:8],
    )


def solution(mesh):
    return jax.shard_map(
        local,
        mesh=mesh,
        in_specs=(
            P("col", ROWS), P(ROWS, None, "col"), P(None, "col"), P(ROWS, "col"), P("col"),
            P(ROWS, "col"), P("col"), P(ROWS, "col"), P("col"), P(None, "col"), P(None, "col"),
            P(ROWS), P(ROWS), P("col", ROWS),
        ),
        out_specs=(
            P("col", ROWS), P("col", ROWS), P(ROWS, None, "col"), P(None, "col"), P(ROWS, "col"),
            P("col"), P(ROWS, "col"), P("col"), P(ROWS, "col"), P("col"), P(None, "col"), P(None, "col"),
        ),
        check_vma=False,
    )
```
